32 devices in a mesh: group: 2 (over x), shard: 16 (over z, y, core).
Axes of the slice: x: 2, y: 2, z: 4, core: 2. Of those that a mesh axis runs over, the one named last changes fastest.
Arguments:
- offer_attribute_matrix: bfloat16 [128, 128, 1024], P(('group', 'shard')), may hold values from -6 to 6
- kept_offers: int32 [128, 32], P(('group', 'shard')), may hold values from 0 to 127, as said below
- expert_target: int32 [128, 6], P(('group', 'shard')), may hold values from 0 to 15, all different within a row; in each aligned block of 4 rows (0 to 3, 4 to 7, ...) at most 3 rows name the same one
- sequence_extent: int32 [128], P(('group', 'shard')), may hold values from 1 to 128
- behaviour_sequence: bfloat16 [128, 128, 512], P(('group', 'shard')), may hold values from -6 to 6
- inner_projection_matrix: bfloat16 [1024, 1024], replicated, may hold values from -0.1875 to 0.1875
- student_rating_vector: bfloat16 [1024], replicated, may hold values from -0.1875 to 0.1875
- asking_matrix: bfloat16 [16, 1024, 512], P('shard'), may hold values from -0.1875 to 0.1875
- lookup_matrix: bfloat16 [16, 512, 512], P('shard'), may hold values from -0.25 to 0.25
- content_matrix: bfloat16 [16, 512, 512], P('shard'), may hold values from -0.25 to 0.25
- expert_rating_vector: bfloat16 [16, 512], P('shard'), may hold values from -1.1953125 to 1.1953125
Outputs:
- grad_hidden: float32 [1024, 1024], P('shard')
- grad_score: float32 [1024], replicated
The draws below stay inside these ranges and needn't reach their ends.
Inputs may be any that keep to these rules, and one draw needn't show every extreme that they name: `kept_offers`: the 32 survivors of a request are distinct candidates. `expert_target`: each request names 6 distinct experts; the requests of one device name any expert at most 3 times, a bound that some block reaches.
All inputs are finite; a program needn't handle non-finite values.
Results may differ from the reference program's by a relative error of at most 0.005.
Values may be sent and summed in bfloat16 or wider, within the bound.
No kernel may reach another device: no remote copies, remote signals or barrier semaphores. Data moves between devices by JAX's collectives and lax.ppermute only.
A program may use at most 128 MiB of HBM per device.

```python
import math
import jax
import jax.numpy as jnp
import numpy as np
from jax import lax

DP = 1024
HP = 1024
ATTENDER_GANGS = 8
DA = 512
CAND = 128
KS = 32
HLEN = 128
TOPR = 6
REQ_DEV = 4
REQUESTS = 128
EXPERTS = 16
CAP = 3
N_GROUP = 2
N_SHARD = 16


def draw_kept_offers(key, part):
    row_keys = jax.random.split(jax.random.fold_in(key, 17), REQUESTS)

    def one_row(row_key):
        return jax.random.permutation(row_key, CAND)[:KS]
    return jax.vmap(one_row)(row_keys).astype(jnp.int32)


def place_ends(entries, stream_key, least, top_value):
    longest = entries.shape.index(max(entries.shape))
    spots = []
    for shift in (0, 1):
        where = [jax.random.randint(jax.random.fold_in(stream_key, axis), (), 0, length) for axis, length in enumerate(entries.shape)]
        where[longest] = (where[longest] + shift) % entries.shape[longest]
        spots.append(tuple(where))
    return entries.at[spots[0]].set(least).at[spots[1]].set(top_value)


def levels(own_key, shape, pieces, least, top_value):
    def one(position, parts):
        heights = jax.random.uniform(jax.random.fold_in(jax.random.fold_in(own_key, 6), position), (parts,), jnp.float32, least / len(pieces), top_value / len(pieces))
        return jnp.repeat(jnp.exp(heights), shape[position] // parts).reshape((-1,) + (1,) * (len(shape) - position - 1))

    level = one(*pieces[0])
    for cut in pieces[1:]:
        level = level * one(*cut)
    return level


def shared_out(own_key, own, number, rows, amount, top, limit, skew):
    sequence = jax.random.permutation(own_key, amount)
    crowded, ordinary = portions_of(amount, rows * top, limit, skew, True), portions_of(amount, rows * top, limit, skew, False)
    places = jnp.arange(amount)

    def named(sizes, rotation):
        used = int((sizes > 0).sum())
        fixed = max(1, used // 4)
        shifted = fixed + (places - fixed + rotation * (used - fixed)) % max(1, amount - fixed)
        return jnp.zeros((amount,), jnp.int32).at[sequence[jnp.where(places < fixed, places, shifted)]].set(jnp.asarray(sizes, jnp.int32))

    sizes = jnp.where(number % 4 == 0, named(crowded, number // 4), named(ordinary, number - number // 4 - 1))
    mixed = jax.random.permutation(jax.random.fold_in(own, 3), amount)
    donor, sink = mixed[0:amount // 2 * 2:2], mixed[1:amount // 2 * 2:2]
    slack = jnp.minimum(sizes[donor] - 1, limit - sizes[sink]) // 2
    slack = jnp.where((donor == sequence[0]) | (sink == sequence[0]) | (sizes[sink] == 0), 0, jnp.maximum(slack, 0))
    shifted = jax.random.randint(jax.random.fold_in(own, 4), (amount // 2,), 0, 1 << 20) % (slack + 1)
    sizes = sizes.at[donor].add(-shifted).at[sink].add(shifted)
    labels = jnp.searchsorted(jnp.cumsum(sizes), jnp.arange(rows * top), side="right").astype(jnp.int32)
    listing = labels.reshape(top, rows).T
    listing = listing[jax.random.permutation(jax.random.fold_in(own, 1), rows)]
    rotation = jax.random.randint(jax.random.fold_in(own, 2), (rows, 1), 0, top)
    return jnp.take_along_axis(listing, (jnp.arange(top)[None, :] + rotation) % top, axis=1)


def portions_of(amount, total, bound, skew, full):
    portions = [(1 << 20) // math.isqrt(grade ** skew) + 1 for grade in range(1, amount + 1)]
    largest = bound if full else min(bound, max(-(-total // amount), total * portions[0] // sum(portions)))
    least = 1 if total - largest >= amount - 1 else 0
    holding, surplus = [largest] + [least] * (amount - 1), total - largest - least * (amount - 1)
    while surplus > 0:
        movable = [i for i in range(1, amount) if holding[i] < largest] or [i for i in range(1, amount) if holding[i] < bound]
        pool, budget = sum([portions[i] for i in movable]), surplus
        for i in movable:
            addition = min(bound - holding[i], max(1, budget * portions[i] // pool), surplus)
            holding[i] = holding[i] + addition
            surplus = surplus - addition
    return np.array(holding)


def centred(own_key, dims, width, reach, cuts=(), held_as=jnp.bfloat16):
    gain = levels(own_key, dims, cuts, -0.22, 0.18) if cuts else 1.0
    drawn = jax.random.normal(own_key, dims, jnp.float32) * width * gain
    return jnp.minimum(jnp.maximum(drawn, -reach), reach).astype(held_as)


def setup_inputs(seed: int = 0) -> dict:
    key_of = jax.random.split(jax.random.key(seed), 12)
    offer_attribute_matrix = centred(key_of[0], (REQUESTS, CAND, DP), 1.0, 6.0, ((0, 32),))
    kept_offers = draw_kept_offers(jax.random.fold_in(key_of[11], 71), 0)
    expert_target_keys = jax.random.split(jax.random.fold_in(key_of[2], 1), REQUESTS // REQ_DEV)
    expert_target_turns = jax.random.permutation(jax.random.fold_in(key_of[2], 3), REQUESTS // REQ_DEV)
    expert_target = jax.vmap(lambda own, number: shared_out(jax.random.fold_in(key_of[2], 2), own, number, REQ_DEV, N_SHARD, TOPR, CAP, 2))(expert_target_keys, expert_target_turns).reshape((REQUESTS, TOPR))
    sequence_extent = place_ends(jax.random.randint(key_of[3], (REQUESTS,), 1, HLEN + 1), jax.random.fold_in(key_of[3], 1), 1, HLEN).astype(jnp.int32)
    behaviour_sequence = centred(key_of[4], (REQUESTS, HLEN, DA), 1.0, 6.0, ((0, 32),))
    inner_projection_matrix = centred(key_of[5], (DP, HP), DP ** -0.5, 0.1875)
    student_rating_vector = centred(key_of[6], (HP,), HP ** -0.5, 0.1875)
    asking_matrix = centred(key_of[7], (EXPERTS, DP, DA), DP ** -0.5, 0.1875, ((0, 16),))
    lookup_matrix = centred(key_of[8], (EXPERTS, DA, DA), DA ** -0.5, 0.25, ((0, 16),))
    content_matrix = centred(key_of[9], (EXPERTS, DA, DA), DA ** -0.5, 0.25, ((0, 16),))
    expert_rating_vector = centred(key_of[10], (EXPERTS, DA), 0.2, 1.1953125, ((0, 16),))
    return {"offer_attribute_matrix": offer_attribute_matrix, "kept_offers": kept_offers, "expert_target": expert_target, "sequence_extent": sequence_extent, "behaviour_sequence": behaviour_sequence, "inner_projection_matrix": inner_projection_matrix, "student_rating_vector": student_rating_vector, "asking_matrix": asking_matrix, "lookup_matrix": lookup_matrix, "content_matrix": content_matrix, "expert_rating_vector": expert_rating_vector}


def teacher_one(selected, history_rows, length, expert, asking_matrix, lookup_matrix, content_matrix, expert_rating_vector):
    queries = jnp.dot(selected, asking_matrix[expert], preferred_element_type=jnp.float32).astype(jnp.bfloat16)
    key_rows = jnp.dot(history_rows, lookup_matrix[expert], preferred_element_type=jnp.float32).astype(jnp.bfloat16)
    value_rows = jnp.dot(history_rows, content_matrix[expert], preferred_element_type=jnp.float32).astype(jnp.bfloat16)
    single_attender_span = queries.shape[1] // ATTENDER_GANGS
    query_heads = queries.reshape(KS, ATTENDER_GANGS, single_attender_span).astype(jnp.float32)
    key_heads = key_rows.reshape(HLEN, ATTENDER_GANGS, single_attender_span).astype(jnp.float32)
    value_heads = value_rows.reshape(HLEN, ATTENDER_GANGS, single_attender_span).astype(jnp.float32)
    logits = jnp.einsum('khd,jhd->hkj', query_heads, key_heads) * (single_attender_span ** -0.5)
    visible = jnp.arange(HLEN, dtype=jnp.int32)[None, None, :] < length
    weights = jnp.where(visible, jnp.exp(logits), jnp.float32(0.0))
    attn_probs = (weights / jnp.sum(weights, axis=-1, keepdims=True)).astype(jnp.bfloat16)
    mixed_context = jnp.einsum('hkj,jhd->khd', attn_probs.astype(jnp.float32), value_heads).reshape(KS, ATTENDER_GANGS * single_attender_span)
    return jnp.sum(mixed_context * expert_rating_vector[expert].astype(jnp.float32), axis=-1)


def reference(offer_attribute_matrix, kept_offers, expert_target, sequence_extent, behaviour_sequence, inner_projection_matrix, student_rating_vector, asking_matrix, lookup_matrix, content_matrix, expert_rating_vector):
    offers_in_segment = REQUESTS // N_GROUP
    score_vec = student_rating_vector.astype(jnp.float32)

    def one_block(totals, group_idx):
        grad_w, grad_s = totals
        first_element = group_idx * offers_in_segment
        features = lax.dynamic_slice_in_dim(offer_attribute_matrix, first_element, offers_in_segment, 0)
        chosen_lines = lax.dynamic_slice_in_dim(kept_offers, first_element, offers_in_segment, 0)
        experts = lax.dynamic_slice_in_dim(expert_target, first_element, offers_in_segment, 0)
        lengths = lax.dynamic_slice_in_dim(sequence_extent, first_element, offers_in_segment, 0)
        history_rows = lax.dynamic_slice_in_dim(behaviour_sequence, first_element, offers_in_segment, 0)
        flat_feats = features.reshape(offers_in_segment * CAND, DP)
        preact = jnp.dot(flat_feats, inner_projection_matrix, preferred_element_type=jnp.float32)
        hidden = jnp.maximum(preact, jnp.float32(0.0))
        scores = jnp.sum(hidden * score_vec, axis=-1).reshape(offers_in_segment, CAND)
        exp_scores = jnp.exp(scores)
        student = exp_scores / jnp.sum(exp_scores, axis=-1, keepdims=True)
        selected = jnp.take_along_axis(features, chosen_lines[:, :, None], axis=1)

        def apply_one(item):
            total = jnp.zeros((KS,), jnp.float32)
            for which in range(TOPR):
                total = total + teacher_one(item[0], item[1], item[2], item[3][which], asking_matrix, lookup_matrix, content_matrix, expert_rating_vector)
            return total / TOPR

        mentor_output = lax.map(apply_one, (selected, history_rows, lengths, experts))
        exp_teacher = jnp.exp(mentor_output)
        target = exp_teacher / jnp.sum(exp_teacher, axis=-1, keepdims=True)
        onehot = (chosen_lines[:, :, None] == jnp.arange(CAND, dtype=jnp.int32)[None, None, :]).astype(jnp.float32)
        target_cand = jnp.sum(target[:, :, None] * onehot, axis=1)
        score_grad = (student - target_cand).reshape(offers_in_segment * CAND, 1)
        hidden_grad = (score_grad * score_vec * (preact > 0).astype(jnp.float32)).astype(jnp.bfloat16)
        grad_w = grad_w + lax.dot_general(flat_feats, hidden_grad, (((0,), (0,)), ((), ())), preferred_element_type=jnp.float32)
        grad_s = grad_s + jnp.sum(score_grad * hidden, axis=0)
        return (grad_w, grad_s), None

    start = (jnp.zeros((DP, HP), jnp.float32), jnp.zeros((HP,), jnp.float32))
    (grad_hidden, grad_score), unused = lax.scan(one_block, start, jnp.arange(N_GROUP, dtype=jnp.int32))
    return grad_hidden, grad_score
```

```python
import functools

import jax
import jax.numpy as jnp
from jax import lax
from jax.experimental import pallas as pl
from jax.experimental.pallas import tpu as pltpu
from jax.sharding import PartitionSpec as P

ATTENDER_GANGS = 8
META_ROWS = 16
VMEM = pltpu.VMEM
F32 = jnp.float32
BF16 = jnp.bfloat16


def full_vmem():
    return pl.BlockSpec(memory_space=pltpu.VMEM)


def rows_of(requests, hist_slots, kept, feature_span, focus_span):
    hist_rows = requests * hist_slots
    kept_rows = requests * kept
    pieces = feature_span // focus_span
    return hist_rows, kept_rows, pieces, hist_rows + kept_rows * pieces


def pack_kernel(x_ref, kept_ref, hist_ref, meta_ref, out_ref):
    requests, cand, _ = x_ref.shape
    kept = kept_ref.shape[1]
    focus = hist_ref.shape[1]
    hist_rows = hist_ref.shape[0]
    pieces = x_ref.shape[2] // focus
    out_ref[:hist_rows, :] = hist_ref[...]
    for r in range(requests):
        cand_of = lax.broadcasted_iota(jnp.int32, (cand, kept), 0)
        pick = (cand_of == kept_ref[r : r + 1, :]).astype(F32).astype(BF16)
        for p in range(pieces):
            rows = lax.dot_general(
                pick,
                x_ref[r, :, p * focus : (p + 1) * focus],
                (((0,), (0,)), ((), ())),
                preferred_element_type=F32,
            )
            at = hist_rows + p * requests * kept + r * kept
            out_ref[at : at + kept, :] = rows.astype(BF16)
    out_ref[hist_rows + pieces * requests * kept :, :] = meta_ref[...]


def pack(x, kept, hist, meta):
    requests, cand, feats = x.shape
    focus = hist.shape[2]
    flat_hist = hist.reshape(-1, focus)
    total = rows_of(requests, hist.shape[1], kept.shape[1], feats, focus)[3] + META_ROWS
    return pl.pallas_call(
        pack_kernel,
        out_shape=jax.ShapeDtypeStruct((total, focus), BF16),
        in_specs=[full_vmem()] * 4,
        out_specs=full_vmem(),
        cost_estimate=pl.CostEstimate(flops=10**8, bytes_accessed=3 * 10**6, transcendentals=0),
    )(x, kept, flat_hist, meta)


def student_kernel(requests, x_ref, w_ref, s_ref, grad_ref, gs_ref, part_ref):
    rows, feats = x_ref.shape
    units = w_ref.shape[1]
    cand = rows // requests
    score_vec = s_ref[...].astype(F32)

    def one(r, total):
        at = pl.ds(pl.multiple_of(r * cand, cand), cand)
        preact = jnp.dot(x_ref[at, :], w_ref[...], preferred_element_type=F32)
        hidden = jnp.maximum(preact, 0.0)
        exp_scores = jnp.exp(jnp.sum(hidden * score_vec, axis=-1, keepdims=True))
        student = exp_scores / jnp.sum(exp_scores, axis=0, keepdims=True)
        live = jnp.where(preact > 0, student * score_vec, 0.0)
        part_ref[at, :] = live.astype(BF16)
        return total + jnp.sum(student * hidden, axis=0, keepdims=True)

    gs_ref[...] = lax.fori_loop(0, requests, one, jnp.zeros((1, units), F32))
    step = min(256, feats)

    def block(i, carry):
        at = pl.ds(pl.multiple_of(i * step, step), step)
        grad_ref[at, :] = lax.dot_general(
            x_ref[:, at], part_ref[...], (((0,), (0,)), ((), ())), preferred_element_type=F32
        )
        return carry

    lax.fori_loop(0, feats // step, block, 0)


def student_part(x, w, s):
    requests, cand, feats = x.shape
    units = w.shape[1]
    return pl.pallas_call(
        functools.partial(student_kernel, requests),
        out_shape=(
            jax.ShapeDtypeStruct((feats, units), F32),
            jax.ShapeDtypeStruct((1, units), F32),
        ),
        in_specs=[full_vmem()] * 3,
        out_specs=(full_vmem(), full_vmem()),
        scratch_shapes=[VMEM((requests * cand, units), BF16)],
        cost_estimate=pl.CostEstimate(
            flops=4 * requests * cand * feats * units, bytes_accessed=8 * 10**6, transcendentals=0
        ),
    )(x.reshape(requests * cand, feats), w, s.reshape(1, units))


def rank_block(dims, me, payload, ask, look, rate, w, sel_rows):
    requests, hist_slots, kept, tops, gangs = dims
    focus = look.shape[0]
    span = look.shape[1] // gangs
    hist_rows, kept_rows, pieces, meta_at = rows_of(
        requests, hist_slots, kept, ask.shape[0], focus
    )
    hist = payload[:hist_rows, :]
    keys = jnp.dot(hist, look[...], preferred_element_type=F32).astype(BF16)
    values = jnp.dot(hist, rate[...], preferred_element_type=F32)
    queries = jnp.zeros((kept_rows, look.shape[1]), F32)
    preact = jnp.zeros((kept_rows, w.shape[1]), F32)
    own = jnp.zeros((sel_rows, kept_rows), F32)
    for p in range(pieces):
        rows = payload[hist_rows + p * kept_rows : hist_rows + (p + 1) * kept_rows, :]
        at = slice(p * focus, (p + 1) * focus)
        queries += jnp.dot(rows, ask[at, :], preferred_element_type=F32)
        preact += jnp.dot(rows, w[at, :], preferred_element_type=F32)
        feature = lax.broadcasted_iota(jnp.int32, (sel_rows, focus), 1) + p * focus
        wanted = lax.broadcasted_iota(jnp.int32, (sel_rows, focus), 0) + me * sel_rows
        pick = (feature == wanted).astype(F32).astype(BF16)
        own += lax.dot_general(pick, rows, (((1,), (1,)), ((), ())), preferred_element_type=F32)
    queries = (queries * span**-0.5).astype(BF16)
    hidden = jnp.maximum(preact, 0.0).astype(BF16)
    wide = gangs * kept
    head_row = lax.broadcasted_iota(jnp.int32, (wide, look.shape[1]), 0) // kept
    head_col = lax.broadcasted_iota(jnp.int32, (wide, look.shape[1]), 1) // span
    same_head = head_row == head_col
    slot = lax.broadcasted_iota(jnp.int32, (hist_slots, wide), 0).astype(F32)
    meta = payload[meta_at : meta_at + META_ROWS, :].astype(F32)
    meta_lane = lax.broadcasted_iota(jnp.int32, meta.shape, 1)
    hit = jnp.where((meta_lane < tops) & (meta == me.astype(F32)), 1.0, 0.0)
    routed = jnp.max(hit, axis=-1, keepdims=True)
    lengths = jnp.sum(jnp.where(meta_lane == tops, meta, 0.0), axis=-1, keepdims=True)
    lane = lax.broadcasted_iota(jnp.int32, (1, kept_rows), 1) // kept
    scores = jnp.zeros((1, kept_rows), F32)
    for r in range(requests):
        q = queries[r * kept : (r + 1) * kept, :]
        q_wide = jnp.where(same_head, jnp.concatenate([q] * gangs, axis=0), jnp.zeros((), BF16))
        logits = lax.dot_general(
            keys[r * hist_slots : (r + 1) * hist_slots, :],
            q_wide,
            (((1,), (1,)), ((), ())),
            preferred_element_type=F32,
        )
        weights = jnp.where(slot < lengths[r : r + 1, :], jnp.exp(logits), 0.0)
        mixed = weights * values[r * hist_slots : (r + 1) * hist_slots, :]
        per_head = jnp.sum(mixed, axis=0, keepdims=True) / jnp.sum(weights, axis=0, keepdims=True)
        folded = per_head[:, :kept_rows]
        for b in range(1, wide // kept_rows):
            folded = folded + per_head[:, b * kept_rows : (b + 1) * kept_rows]
        shift = kept
        while shift < kept_rows:
            folded = folded + pltpu.roll(folded, shift, 1)
            shift *= 2
        scores = jnp.where(lane == r, folded * routed[r : r + 1, :], scores)
    return scores, hidden, own.astype(BF16)


def rank_kernel(dims, sel_rows, me_ref, p_ref, a_ref, l_ref, r_ref, w_ref, o_ref, h_ref, s_ref):
    scores, hidden, own = rank_block(
        dims, me_ref[0], p_ref.at[0], a_ref, l_ref, r_ref, w_ref, sel_rows
    )
    o_ref[0] = scores
    h_ref[...] = hidden
    s_ref[...] = own


def rank(dims, me, payloads, ask, look, rate, w, sel_rows):
    blocks, rows, focus = payloads.shape
    requests, hist_slots, kept, _, _ = dims
    kept_rows = requests * kept
    units = w.shape[1]
    hold = dict(pipeline_mode=pl.Buffered(1))
    return pl.pallas_call(
        functools.partial(rank_kernel, dims, sel_rows),
        out_shape=(
            jax.ShapeDtypeStruct((blocks, 1, kept_rows), F32),
            jax.ShapeDtypeStruct((blocks * kept_rows, units), BF16),
            jax.ShapeDtypeStruct((sel_rows, blocks * kept_rows), BF16),
        ),
        grid=(blocks,),
        in_specs=[
            pl.BlockSpec(memory_space=pltpu.SMEM),
            pl.BlockSpec((1, rows, focus), lambda b: (b, 0, 0)),
            pl.BlockSpec(ask.shape, lambda b: (0, 0), **hold),
            pl.BlockSpec(look.shape, lambda b: (0, 0), **hold),
            pl.BlockSpec(rate.shape, lambda b: (0, 0), **hold),
            pl.BlockSpec(w.shape, lambda b: (0, 0), **hold),
        ],
        out_specs=(
            pl.BlockSpec((1, 1, kept_rows), lambda b: (b, 0, 0)),
            pl.BlockSpec((kept_rows, units), lambda b: (b, 0)),
            pl.BlockSpec((sel_rows, kept_rows), lambda b: (0, b)),
        ),
        cost_estimate=pl.CostEstimate(
            flops=blocks * 10**9, bytes_accessed=blocks * 10**6, transcendentals=0
        ),
    )(me, payloads, ask, look, rate, w)


def target_kernel(kept, tops, got_ref, hid_ref, sel_ref, s_ref, base_ref, out_ref):
    blocks, kept_rows = got_ref.shape[1] - s_ref.shape[1] // got_ref.shape[2], got_ref.shape[2]
    sel_rows = sel_ref.shape[0]
    units = s_ref.shape[1]
    total = jnp.sum(got_ref[...], axis=0)
    exp_teacher = jnp.exp(total[:blocks, :] / tops)
    near = lax.broadcasted_iota(jnp.int32, (kept_rows, kept_rows), 0) // kept
    far = lax.broadcasted_iota(jnp.int32, (kept_rows, kept_rows), 1) // kept
    group = (near == far).astype(F32)
    sums = jnp.dot(
        exp_teacher, group, preferred_element_type=F32, precision=lax.Precision.HIGHEST
    )
    target = exp_teacher / sums
    high = target.astype(BF16)
    low = (target - high.astype(F32)).astype(BF16)
    grad = jnp.zeros((sel_rows, units), F32)
    lift = jnp.zeros((1, units), F32)
    for b in range(blocks):
        at = slice(b * kept_rows, (b + 1) * kept_rows)
        hidden = hid_ref[at, :]
        live = jnp.where(hidden > 0, jnp.ones((), BF16), jnp.zeros((), BF16))
        scaled = (sel_ref[:, at].astype(F32) * target[b : b + 1, :]).astype(BF16)
        grad += jnp.dot(scaled, live, preferred_element_type=F32)
        both = jnp.concatenate([high[b : b + 1, :], low[b : b + 1, :]], axis=0)
        pair = jnp.dot(both, hidden, preferred_element_type=F32)
        lift += pair[0:1, :] + pair[1:2, :]
    out_ref[:sel_rows, :] = base_ref[...] - grad * s_ref[...].astype(F32)
    lanes = got_ref.shape[2]
    for i in range(units // lanes):
        at = slice(i * lanes, (i + 1) * lanes)
        out_ref[sel_rows : sel_rows + 1, at] = total[blocks + i : blocks + i + 1, :] - lift[:, at]
    out_ref[sel_rows + 1 :, :] = jnp.zeros((out_ref.shape[0] - sel_rows - 1, units), F32)


def target_part(kept, tops, got, hidden, own, s, base):
    sel_rows = own.shape[0]
    units = hidden.shape[1]
    return pl.pallas_call(
        functools.partial(target_kernel, kept, tops),
        out_shape=jax.ShapeDtypeStruct((sel_rows + 8, units), F32),
        in_specs=[full_vmem()] * 5,
        out_specs=full_vmem(),
        cost_estimate=pl.CostEstimate(flops=10**9, bytes_accessed=6 * 10**6, transcendentals=0),
    )(got, hidden, own, s.reshape(1, units), base)


def body(
    offer_attribute_matrix,
    kept_offers,
    expert_target,
    sequence_extent,
    behaviour_sequence,
    inner_projection_matrix,
    student_rating_vector,
    asking_matrix,
    lookup_matrix,
    content_matrix,
    expert_rating_vector,
):
    requests, _, feats = offer_attribute_matrix.shape
    kept = kept_offers.shape[1]
    hist_slots, focus = behaviour_sequence.shape[1:]
    tops = expert_target.shape[1]
    units = inner_projection_matrix.shape[1]
    n_shard = lax.axis_size("shard")
    sel_rows = feats // n_shard
    kept_rows = requests * kept
    me = lax.axis_index("shard")

    meta = jnp.concatenate([expert_target, sequence_extent[:, None]], axis=1).astype(BF16)
    meta = jnp.pad(meta, ((0, META_ROWS - requests), (0, focus - tops - 1)))
    payload = pack(offer_attribute_matrix, kept_offers, behaviour_sequence, meta)
    payloads = lax.all_gather(payload, "shard", axis=0, tiled=False)

    grad_student, gs_student = student_part(
        offer_attribute_matrix, inner_projection_matrix, student_rating_vector
    )
    base = lax.psum_scatter(grad_student, "shard", scatter_dimension=0, tiled=True)

    head_of = jnp.arange(focus, dtype=jnp.int32)[:, None] // (focus // ATTENDER_GANGS)
    lane_head = jnp.arange(ATTENDER_GANGS * kept, dtype=jnp.int32)[None, :] // kept
    rated = content_matrix[0].astype(F32) * expert_rating_vector[0].astype(F32)
    rate = jnp.dot(
        rated, (head_of == lane_head).astype(F32), precision=lax.Precision.HIGHEST
    ).astype(BF16)

    dims = (requests, hist_slots, kept, tops, ATTENDER_GANGS)
    scores, hidden, own = rank(
        dims,
        me.reshape(1).astype(jnp.int32),
        payloads,
        asking_matrix[0],
        lookup_matrix[0],
        rate,
        inner_projection_matrix,
        sel_rows,
    )
    lanes = kept_rows
    send = jnp.concatenate([scores.reshape(-1, lanes), gs_student.reshape(-1, lanes)], axis=0)
    send = jnp.broadcast_to(send[None], (n_shard,) + send.shape)
    got = lax.all_to_all(send, "shard", split_axis=0, concat_axis=0, tiled=True)
    mine = target_part(kept, tops, got, hidden, own, student_rating_vector, base)
    whole = lax.psum(mine, "group")
    return whole[:sel_rows], whole[sel_rows]


def solution(mesh):
    placed = (
        P(("group", "shard"), None, None),
        P(("group", "shard"), None),
        P(("group", "shard"), None),
        P(("group", "shard")),
        P(("group", "shard"), None, None),
        P(),
        P(),
        P("shard", None, None),
        P("shard", None, None),
        P("shard", None, None),
        P("shard", None),
    )
    return jax.shard_map(
        body, mesh=mesh, in_specs=placed, out_specs=(P("shard", None), P()), check_vma=False
    )
```

```python
import functools

import jax
import jax.numpy as jnp
from jax import lax
from jax.experimental import pallas as pl
from jax.experimental.pallas import tpu as pltpu
from jax.sharding import PartitionSpec as P

ATTENDER_GANGS = 8
META_ROWS = 16
VMEM = pltpu.VMEM
F32 = jnp.float32
BF16 = jnp.bfloat16


def full_vmem():
    return pl.BlockSpec(memory_space=pltpu.VMEM)


def rows_of(requests, hist_slots, kept, feature_span, focus_span):
    hist_rows = requests * hist_slots
    kept_rows = requests * kept
    pieces = feature_span // focus_span
    return hist_rows, kept_rows, pieces, hist_rows + kept_rows * pieces


def pack_kernel(x_ref, kept_ref, hist_ref, meta_ref, out_ref):
    requests, cand, _ = x_ref.shape
    kept = kept_ref.shape[1]
    focus = hist_ref.shape[1]
    hist_rows = hist_ref.shape[0]
    pieces = x_ref.shape[2] // focus
    out_ref[:hist_rows, :] = hist_ref[...]
    for r in range(requests):
        cand_of = lax.broadcasted_iota(jnp.int32, (cand, kept), 0)
        pick = (cand_of == kept_ref[r : r + 1, :]).astype(F32).astype(BF16)
        for p in range(pieces):
            rows = lax.dot_general(
                pick,
                x_ref[r, :, p * focus : (p + 1) * focus],
                (((0,), (0,)), ((), ())),
                preferred_element_type=F32,
            )
            at = hist_rows + p * requests * kept + r * kept
            out_ref[at : at + kept, :] = rows.astype(BF16)
    out_ref[hist_rows + pieces * requests * kept :, :] = meta_ref[...]


def pack(x, kept, hist, meta):
    requests, cand, feats = x.shape
    focus = hist.shape[2]
    flat_hist = hist.reshape(-1, focus)
    total = rows_of(requests, hist.shape[1], kept.shape[1], feats, focus)[3] + META_ROWS
    return pl.pallas_call(
        pack_kernel,
        out_shape=jax.ShapeDtypeStruct((total, focus), BF16),
        in_specs=[full_vmem()] * 4,
        out_specs=full_vmem(),
        cost_estimate=pl.CostEstimate(flops=10**8, bytes_accessed=3 * 10**6, transcendentals=0),
    )(x, kept, flat_hist, meta)


def student_kernel(requests, chunk, order, me_ref, x_ref, w_ref, s_ref, *refs):
    grad_refs, (gs_ref, part_ref) = refs[:-2], refs[-2:]
    rows, feats = x_ref.shape
    units = w_ref.shape[1]
    cand = rows // requests
    score_vec = s_ref[...].astype(F32)

    def one(r, total):
        at = pl.ds(pl.multiple_of(r * cand, cand), cand)
        preact = jnp.dot(x_ref[at, :], w_ref[...], preferred_element_type=F32)
        hidden = jnp.maximum(preact, 0.0)
        exp_scores = jnp.exp(jnp.sum(hidden * score_vec, axis=-1, keepdims=True))
        student = exp_scores / jnp.sum(exp_scores, axis=0, keepdims=True)
        live = jnp.where(preact > 0, student * score_vec, 0.0)
        part_ref[at, :] = live.astype(BF16)
        return total + jnp.sum(student * hidden, axis=0, keepdims=True)

    gs_ref[...] = lax.fori_loop(0, requests, one, jnp.zeros((1, units), F32))
    step = min(256, feats)

    held = grad_refs[0].shape[0] // chunk

    def block(i, carry):
        at = pl.ds(pl.multiple_of(i * step, step), step)
        grad = lax.dot_general(
            x_ref[:, at], part_ref[...], (((0,), (0,)), ((), ())), preferred_element_type=F32
        )
        for j in range(step // chunk):
            piece = grad[j * chunk : (j + 1) * chunk, :]
            spot = order(i * (step // chunk) + j, me_ref[0])
            if len(grad_refs) == 1:
                grad_refs[0][pl.ds(pl.multiple_of(spot * chunk, chunk), chunk), :] = piece
            else:
                for half, ref in enumerate(grad_refs):

                    @pl.when(spot // held == half)
                    def _(ref=ref, half=half, piece=piece, spot=spot):
                        place = jnp.clip(spot - half * held, 0, held - 1)
                        ref[pl.ds(pl.multiple_of(place * chunk, chunk), chunk), :] = piece

        return carry

    lax.fori_loop(0, feats // step, block, 0)


def student_part(x, w, s, me, pieces, halves, order):
    requests, cand, feats = x.shape
    units = w.shape[1]
    return pl.pallas_call(
        functools.partial(student_kernel, requests, feats // pieces, order),
        out_shape=(jax.ShapeDtypeStruct((feats // halves, units), F32),) * halves
        + (jax.ShapeDtypeStruct((1, units), F32),),
        in_specs=[pl.BlockSpec(memory_space=pltpu.SMEM)] + [full_vmem()] * 3,
        out_specs=(full_vmem(),) * (halves + 1),
        scratch_shapes=[VMEM((requests * cand, units), BF16)],
        cost_estimate=pl.CostEstimate(
            flops=4 * requests * cand * feats * units, bytes_accessed=8 * 10**6, transcendentals=0
        ),
    )(me, x.reshape(requests * cand, feats), w, s.reshape(1, units))


def block_scores(dims, me, payload, ask, look, rate):
    requests, hist_slots, kept, tops, gangs = dims
    focus = look.shape[0]
    span = look.shape[1] // gangs
    hist_rows, kept_rows, pieces, meta_at = rows_of(
        requests, hist_slots, kept, ask.shape[0], focus
    )
    hist = payload[:hist_rows, :]
    keys = jnp.dot(hist, look[...], preferred_element_type=F32).astype(BF16)
    values = jnp.dot(hist, rate[...], preferred_element_type=F32)
    queries = jnp.zeros((kept_rows, look.shape[1]), F32)
    for p in range(pieces):
        rows = payload[hist_rows + p * kept_rows : hist_rows + (p + 1) * kept_rows, :]
        at = slice(p * focus, (p + 1) * focus)
        queries += jnp.dot(rows, ask[at, :], preferred_element_type=F32)
    queries = (queries * span**-0.5).astype(BF16)
    wide = gangs * kept
    head_row = lax.broadcasted_iota(jnp.int32, (wide, look.shape[1]), 0) // kept
    head_col = lax.broadcasted_iota(jnp.int32, (wide, look.shape[1]), 1) // span
    same_head = head_row == head_col
    slot = lax.broadcasted_iota(jnp.int32, (hist_slots, wide), 0).astype(F32)
    meta = payload[meta_at : meta_at + META_ROWS, :].astype(F32)
    meta_lane = lax.broadcasted_iota(jnp.int32, meta.shape, 1)
    hit = jnp.where((meta_lane < tops) & (meta == me.astype(F32)), 1.0, 0.0)
    routed = jnp.max(hit, axis=-1, keepdims=True)
    lengths = jnp.sum(jnp.where(meta_lane == tops, meta, 0.0), axis=-1, keepdims=True)
    lane = lax.broadcasted_iota(jnp.int32, (1, kept_rows), 1) // kept
    scores = jnp.zeros((1, kept_rows), F32)
    for r in range(requests):
        q = queries[r * kept : (r + 1) * kept, :]
        q_wide = jnp.where(same_head, jnp.concatenate([q] * gangs, axis=0), jnp.zeros((), BF16))
        logits = lax.dot_general(
            keys[r * hist_slots : (r + 1) * hist_slots, :],
            q_wide,
            (((1,), (1,)), ((), ())),
            preferred_element_type=F32,
        )
        weights = jnp.where(slot < lengths[r : r + 1, :], jnp.exp(logits), 0.0)
        mixed = weights * values[r * hist_slots : (r + 1) * hist_slots, :]
        per_head = jnp.sum(mixed, axis=0, keepdims=True) / jnp.sum(weights, axis=0, keepdims=True)
        folded = per_head[:, :kept_rows]
        for b in range(1, wide // kept_rows):
            folded = folded + per_head[:, b * kept_rows : (b + 1) * kept_rows]
        shift = kept
        while shift < kept_rows:
            folded = folded + pltpu.roll(folded, shift, 1)
            shift *= 2
        scores = jnp.where((lane == r) & (routed[r : r + 1, :] > 0), folded, scores)
    return scores


def block_hidden(dims, me, payload, w, sel_rows):
    requests, hist_slots, kept, _, _ = dims
    focus = payload.shape[1]
    hist_rows, kept_rows, pieces, _ = rows_of(requests, hist_slots, kept, w.shape[0], focus)
    preact = jnp.zeros((kept_rows, w.shape[1]), F32)
    own = jnp.zeros((sel_rows, kept_rows), F32)
    for p in range(pieces):
        rows = payload[hist_rows + p * kept_rows : hist_rows + (p + 1) * kept_rows, :]
        at = slice(p * focus, (p + 1) * focus)
        preact += jnp.dot(rows, w[at, :], preferred_element_type=F32)
        feature = lax.broadcasted_iota(jnp.int32, (sel_rows, focus), 1) + p * focus
        wanted = lax.broadcasted_iota(jnp.int32, (sel_rows, focus), 0) + me * sel_rows
        pick = (feature == wanted).astype(F32).astype(BF16)
        own += lax.dot_general(pick, rows, (((1,), (1,)), ((), ())), preferred_element_type=F32)
    return jnp.maximum(preact, 0.0).astype(BF16), own.astype(BF16)


def rank_kernel(dims, sel_rows, layout, wants, me_ref, *refs):
    n_in = sum(layout) if layout else 1
    arrays, refs = refs[:n_in], refs[n_in:]
    if wants[0]:
        (a_ref, l_ref, r_ref), refs = refs[:3], refs[3:]
    if wants[1]:
        (w_ref,), refs = refs[:1], refs[1:]
    if wants[0]:
        (o_ref,), refs = refs[:1], refs[1:]
    if wants[1]:
        (h_ref, s_ref), refs = refs[:2], refs[2:]
    if layout:
        buf, sems = refs
        step = pl.program_id(0)

        @pl.when(step == 0)
        def _():
            i = 0
            for b, count in enumerate(layout):
                at = 0
                for _ in range(count):
                    rows = arrays[i].shape[0]
                    pltpu.make_async_copy(
                        arrays[i], buf.at[b, pl.ds(at, rows), :], sems.at[b]
                    ).start()
                    at += rows
                    i += 1

        pltpu.make_async_copy(buf.at[step], buf.at[step], sems.at[step]).wait()
        payload = buf.at[step]
    else:
        payload = arrays[0].at[0]
    me = me_ref[0]
    if wants[0]:
        o_ref[0] = block_scores(dims, me, payload, a_ref, l_ref, r_ref)
    if wants[1]:
        h_ref[...], s_ref[...] = block_hidden(dims, me, payload, w_ref, sel_rows)


def rank(dims, me, payloads, score_weights, hidden_weights, sel_rows):
    requests, hist_slots, kept, _, _ = dims
    kept_rows = requests * kept
    stacked = not isinstance(payloads, list)
    hold = dict(pipeline_mode=pl.Buffered(1))
    if stacked:
        blocks, rows, focus = payloads.shape
        layout, arrays, scratch = None, [payloads], []
        specs = [pl.BlockSpec((1, rows, focus), lambda b: (b, 0, 0))]
    else:
        blocks = len(payloads)
        layout = [len(p) for p in payloads]
        arrays = [a for p in payloads for a in p]
        rows, focus = sum(a.shape[0] for a in payloads[0]), arrays[0].shape[1]
        specs = [pl.BlockSpec(memory_space=pl.ANY)] * len(arrays)
        scratch = [VMEM((blocks, rows, focus), BF16), pltpu.SemaphoreType.DMA((blocks,))]
    wants = (score_weights is not None, hidden_weights is not None)
    weights = list(score_weights or ()) + list(hidden_weights or ())
    shapes, outs = [], []
    if wants[0]:
        shapes.append(jax.ShapeDtypeStruct((blocks, 1, kept_rows), F32))
        outs.append(pl.BlockSpec((1, 1, kept_rows), lambda b: (b, 0, 0)))
    if wants[1]:
        units = hidden_weights[0].shape[1]
        shapes.append(jax.ShapeDtypeStruct((blocks * kept_rows, units), BF16))
        outs.append(pl.BlockSpec((kept_rows, units), lambda b: (b, 0)))
        shapes.append(jax.ShapeDtypeStruct((sel_rows, blocks * kept_rows), BF16))
        outs.append(pl.BlockSpec((sel_rows, kept_rows), lambda b: (0, b)))
    return pl.pallas_call(
        functools.partial(rank_kernel, dims, sel_rows, layout, wants),
        out_shape=tuple(shapes),
        grid=(blocks,),
        in_specs=[pl.BlockSpec(memory_space=pltpu.SMEM)]
        + specs
        + [pl.BlockSpec(m.shape, lambda b: (0, 0), **hold) for m in weights],
        out_specs=tuple(outs),
        scratch_shapes=scratch,
        cost_estimate=pl.CostEstimate(
            flops=blocks * 10**9, bytes_accessed=blocks * 10**6, transcendentals=0
        ),
    )(me, *arrays, *weights)


def send_kernel(parts, n_score, me_ref, *refs):
    score_refs, gs_ref, out_ref = refs[:n_score], refs[n_score], refs[n_score + 1]
    peers, rows, lanes = out_ref.shape
    blocks = sum(parts)
    slot = 0
    for ref, count in zip(score_refs, parts):
        for b in range(count):
            row = ref[b]
            out_ref[:, pl.ds(me_ref[1] ^ slot, 1), :] = jnp.broadcast_to(
                row[None], (peers, 1, lanes)
            )
            slot += 1
    for i in range(rows - blocks):
        row = gs_ref[:, i * lanes : (i + 1) * lanes]
        out_ref[:, blocks + i : blocks + i + 1, :] = jnp.broadcast_to(row[None], (peers, 1, lanes))


def message(me, scores, gs, peers):
    parts = [s.shape[0] for s in scores]
    lanes = scores[0].shape[-1]
    rows = sum(parts) + gs.shape[1] // lanes
    return pl.pallas_call(
        functools.partial(send_kernel, parts, len(scores)),
        out_shape=jax.ShapeDtypeStruct((peers, rows, lanes), F32),
        in_specs=[pl.BlockSpec(memory_space=pltpu.SMEM)] + [full_vmem()] * (len(scores) + 1),
        out_specs=full_vmem(),
    )(me, *scores, gs)


def target_kernel(kept, tops, n_parts, me_ref, got_ref, s_ref, base_ref, *refs):
    hid_refs, sel_refs = refs[:n_parts], refs[n_parts : 2 * n_parts]
    out_ref, target_ref = refs[2 * n_parts :]
    kept_rows = got_ref.shape[2]
    units = s_ref.shape[1]
    blocks = got_ref.shape[1] - units // kept_rows
    sel_rows = sel_refs[0].shape[0]
    total = jnp.sum(got_ref[...], axis=0)
    exp_teacher = jnp.exp(total[:blocks, :] / tops)
    near = lax.broadcasted_iota(jnp.int32, (kept_rows, kept_rows), 0) // kept
    far = lax.broadcasted_iota(jnp.int32, (kept_rows, kept_rows), 1) // kept
    group = (near == far).astype(F32)
    sums = jnp.dot(
        exp_teacher, group, preferred_element_type=F32, precision=lax.Precision.HIGHEST
    )
    target_ref[...] = exp_teacher / sums
    grad = jnp.zeros((sel_rows, units), F32)
    lift = jnp.zeros((1, units), F32)
    slot = 0
    for hid_ref, sel_ref in zip(hid_refs, sel_refs):
        for b in range(hid_ref.shape[0] // kept_rows):
            at = slice(b * kept_rows, (b + 1) * kept_rows)
            target = target_ref[pl.ds(me_ref[1] ^ slot, 1), :]
            high = target.astype(BF16).astype(F32)
            hidden = hid_ref[at, :]
            live = jnp.where(hidden > 0, jnp.ones((), BF16), jnp.zeros((), BF16))
            scaled = (sel_ref[:, at].astype(F32) * target).astype(BF16)
            grad += jnp.dot(scaled, live, preferred_element_type=F32)
            both = jnp.concatenate([high, target - high], axis=0).astype(BF16)
            pair = jnp.dot(both, hidden, preferred_element_type=F32)
            lift += pair[0:1, :] + pair[1:2, :]
            slot += 1
    out_ref[:sel_rows, :] = -grad * s_ref[...].astype(F32)
    held = base_ref.shape[0]
    at = pl.ds(pl.multiple_of(me_ref[2] * held, 8), held)
    out_ref[at, :] = out_ref[at, :] + base_ref[...]
    for i in range(units // kept_rows):
        at = slice(i * kept_rows, (i + 1) * kept_rows)
        out_ref[sel_rows : sel_rows + 1, at] = total[blocks + i : blocks + i + 1, :] - lift[:, at]
    out_ref[sel_rows + 1 :, :] = jnp.zeros((out_ref.shape[0] - sel_rows - 1, units), F32)


def target_part(kept, tops, me, got, hiddens, owns, s, base):
    sel_rows = owns[0].shape[0]
    units = hiddens[0].shape[1]
    blocks = got.shape[1] - units // got.shape[2]
    return pl.pallas_call(
        functools.partial(target_kernel, kept, tops, len(hiddens)),
        out_shape=jax.ShapeDtypeStruct((sel_rows + 8, units), F32),
        in_specs=[pl.BlockSpec(memory_space=pltpu.SMEM)] + [full_vmem()] * (3 + 2 * len(hiddens)),
        out_specs=full_vmem(),
        scratch_shapes=[VMEM((blocks, got.shape[2]), F32)],
        cost_estimate=pl.CostEstimate(flops=10**9, bytes_accessed=6 * 10**6, transcendentals=0),
    )(me, got, s.reshape(1, units), base, *hiddens, *owns)


def along(pairs):
    table = []
    for z, z_to in pairs:
        for low in range(4):
            table.append((4 * z + low, 4 * z_to + low))
    return table


def flip(bits):
    return [(i, i ^ bits) for i in range(16)]


SIBLING, Y_OVER, Z_NEAR, Z_FAR = flip(1), flip(2), flip(4), flip(8)
Z_INNER = along([(1, 2), (2, 1)])
Z_OUT = along([(1, 0), (2, 3)])


def shift(x, table, axis="shard"):
    return lax.ppermute(x, axis, table)


def gather_stages(b, me):
    inner = ((me >> 2) ^ (me >> 3)) & 1 == 1
    cut = -(-b.shape[0] // 32) * 16
    near = shift(b, Z_NEAR)
    mid = shift(b, Z_INNER)
    over = shift(b, Y_OVER)
    mid_far = shift(near, Z_INNER)
    out_far = shift(mid, Z_OUT)
    over_near = shift(near, Y_OVER)
    far = jnp.where(inner, mid_far, out_far)
    out_last = shift(mid_far, Z_OUT)
    over_far = shift(far, Y_OVER)
    last = jnp.where(inner, mid, out_last)
    over_last = shift(last[:cut], Y_OVER)
    rest_out = shift(over_far[cut:], Z_OUT)
    rest_mid = shift(over[cut:], Z_INNER)
    over_rest = jnp.where(inner, rest_mid, rest_out)

    def both(*pieces):
        return [list(pieces), [shift(p, SIBLING) for p in pieces]]

    return [
        both(b),
        both(over) + both(near),
        both(over_near) + both(far),
        both(over_far) + both(last),
        both(over_last, over_rest),
    ]


def halving_order(block, me):
    away = block ^ me
    z1, z0, y, core, grp = [(away >> i) & 1 for i in (4, 3, 2, 1, 0)]
    return (core << 4) | (grp << 3) | (z0 << 2) | (z1 << 1) | y


def halve(keep, sent):
    for table, axis in (
        (SIBLING, "shard"),
        ([(0, 1), (1, 0)], "group"),
        (Z_NEAR, "shard"),
        (Z_FAR, "shard"),
        (Y_OVER, "shard"),
    ):
        got = shift(sent, table, axis)
        half = keep.shape[0] // 2
        if table is Y_OVER:
            return keep + got
        keep, sent = keep[:half] + got[:half], keep[half:] + got[half:]


def body(
    offer_attribute_matrix,
    kept_offers,
    expert_target,
    sequence_extent,
    behaviour_sequence,
    inner_projection_matrix,
    student_rating_vector,
    asking_matrix,
    lookup_matrix,
    content_matrix,
    expert_rating_vector,
):
    requests, _, feats = offer_attribute_matrix.shape
    kept = kept_offers.shape[1]
    hist_slots, focus = behaviour_sequence.shape[1:]
    tops = expert_target.shape[1]
    units = inner_projection_matrix.shape[1]
    n_shard = lax.axis_size("shard")
    sel_rows = feats // n_shard
    kept_rows = requests * kept
    me = lax.axis_index("shard")
    n_group = lax.axis_size("group")
    grp = lax.axis_index("group")

    meta = jnp.concatenate([expert_target, sequence_extent[:, None]], axis=1).astype(BF16)
    meta = jnp.pad(meta, ((0, META_ROWS - requests), (0, focus - tops - 1)))
    payload = pack(offer_attribute_matrix, kept_offers, behaviour_sequence, meta)

    linked = n_shard == 16 and n_group == 2
    place = (me * n_group + grp).astype(jnp.int32) if linked else me
    stack = (offer_attribute_matrix, inner_projection_matrix, student_rating_vector)
    if linked:
        stages = gather_stages(payload, me)
        keep, sent, gs_student = student_part(
            *stack, place.reshape(1), n_shard * n_group, 2, halving_order
        )
        base = halve(keep, sent)
        info = jnp.stack([me, me, grp]).astype(jnp.int32)
    else:
        stages = [lax.all_gather(payload, "shard", axis=0, tiled=False)]
        grad_student, gs_student = student_part(
            *stack, place.reshape(1), n_shard, 1, lambda block, at: block
        )
        base = lax.psum_scatter(grad_student, "shard", scatter_dimension=0, tiled=True)
        info = jnp.stack([me, 0 * me, 0 * me]).astype(jnp.int32)

    head_of = jnp.arange(focus, dtype=jnp.int32)[:, None] // (focus // ATTENDER_GANGS)
    lane_head = jnp.arange(ATTENDER_GANGS * kept, dtype=jnp.int32)[None, :] // kept
    rated = content_matrix[0].astype(F32) * expert_rating_vector[0].astype(F32)
    rate = jnp.dot(
        rated, (head_of == lane_head).astype(F32), precision=lax.Precision.HIGHEST
    ).astype(BF16)

    dims = (requests, hist_slots, kept, tops, ATTENDER_GANGS)
    score_weights = (asking_matrix[0], lookup_matrix[0], rate)
    hidden_weights = (inner_projection_matrix,)
    scores, hiddens, owns = [], [], []
    for stage in stages[:-1]:
        score, hidden, own = rank(dims, info, stage, score_weights, hidden_weights, sel_rows)
        scores.append(score)
        hiddens.append(hidden)
        owns.append(own)
    scores.append(rank(dims, info, stages[-1], score_weights, None, sel_rows)[0])
    hidden, own = rank(dims, info, stages[-1], None, hidden_weights, sel_rows)
    hiddens.append(hidden)
    owns.append(own)
    send = message(info, scores, gs_student, n_shard)
    got = lax.all_to_all(send, "shard", split_axis=0, concat_axis=0, tiled=True)
    mine = target_part(kept, tops, info, got, hiddens, owns, student_rating_vector, base)
    if linked:
        whole = mine + shift(mine, [(0, 1), (1, 0)], "group")
    else:
        whole = lax.psum(mine, "group")
    return whole[:sel_rows], whole[sel_rows]


def solution(mesh):
    placed = (
        P(("group", "shard"), None, None),
        P(("group", "shard"), None),
        P(("group", "shard"), None),
        P(("group", "shard")),
        P(("group", "shard"), None, None),
        P(),
        P(),
        P("shard", None, None),
        P("shard", None, None),
        P("shard", None, None),
        P("shard", None),
    )
    return jax.shard_map(
        body, mesh=mesh, in_specs=placed, out_specs=(P("shard", None), P()), check_vma=False
    )
```

```python
import functools

import jax
import jax.numpy as jnp
from jax import lax
from jax.experimental import pallas as pl
from jax.experimental.pallas import tpu as pltpu
from jax.sharding import PartitionSpec as P


ATTENDER_GANGS = 8
META_ROWS = 16
VMEM = pltpu.VMEM
F32 = jnp.float32
BF16 = jnp.bfloat16


def full_vmem():
    return pl.BlockSpec(memory_space=pltpu.VMEM)


def in_place():
    return pl.BlockSpec(memory_space=pl.ANY)


def scalars():
    return pl.BlockSpec(memory_space=pltpu.SMEM)


def room(mib):
    return pltpu.CompilerParams(vmem_limit_bytes=mib * 2**20)


def stays(x):
    return pltpu.with_memory_space_constraint(x, pltpu.HBM)


def fetch(source, target, sem):
    copy = pltpu.make_async_copy(source, target, sem)
    copy.start()
    return copy.wait


def rows_of(requests, hist_slots, kept, feature_span, focus_span):
    hist_rows = requests * hist_slots
    kept_rows = requests * kept
    pieces = feature_span // focus_span
    return hist_rows, kept_rows, pieces, hist_rows + kept_rows * pieces


def pack_kernel(target_ref, extent_ref, x_hbm, kept_ref, hist_hbm, out_ref, x_ref, sems):
    requests, cand, _ = x_ref.shape
    kept = kept_ref.shape[1]
    focus = hist_hbm.shape[1]
    hist_rows = hist_hbm.shape[0]
    tops = target_ref.shape[1]
    pieces = x_ref.shape[2] // focus
    meta_at = hist_rows + pieces * requests * kept
    waits = [fetch(x_hbm.at[r], x_ref.at[r], sems.at[r]) for r in range(requests)]
    wait_hist = fetch(hist_hbm, out_ref.at[pl.ds(0, hist_rows), :], sems.at[requests])
    row = lax.broadcasted_iota(jnp.int32, (META_ROWS, focus), 0)
    lane = lax.broadcasted_iota(jnp.int32, (META_ROWS, focus), 1)
    meta = jnp.zeros((META_ROWS, focus), jnp.int32)
    for r in range(requests):
        for t in range(tops):
            meta = jnp.where((row == r) & (lane == t), target_ref[r, t], meta)
        meta = jnp.where((row == r) & (lane == tops), extent_ref[r], meta)
    out_ref[meta_at:, :] = meta.astype(F32).astype(BF16)
    for r in range(requests):
        waits[r]()
        cand_of = lax.broadcasted_iota(jnp.int32, (cand, kept), 0)
        pick = (cand_of == kept_ref[r : r + 1, :]).astype(F32).astype(BF16)
        for p in range(pieces):
            rows = lax.dot_general(
                pick,
                x_ref[r, :, p * focus : (p + 1) * focus],
                (((0,), (0,)), ((), ())),
                preferred_element_type=F32,
            )
            at = hist_rows + p * requests * kept + r * kept
            out_ref[at : at + kept, :] = rows.astype(BF16)
    wait_hist()


def pack(x, kept, hist, targets, extents):
    requests, _, feats = x.shape
    focus = hist.shape[2]
    flat_hist = hist.reshape(-1, focus)
    total = rows_of(requests, hist.shape[1], kept.shape[1], feats, focus)[3] + META_ROWS
    return pl.pallas_call(
        pack_kernel,
        out_shape=jax.ShapeDtypeStruct((total, focus), BF16),
        in_specs=[scalars(), scalars(), in_place(), full_vmem(), in_place()],
        out_specs=full_vmem(),
        scratch_shapes=[VMEM(x.shape, BF16), pltpu.SemaphoreType.DMA((requests + 1,))],
        cost_estimate=pl.CostEstimate(flops=10**8, bytes_accessed=3 * 10**6, transcendentals=0),
    )(targets, extents, stays(x), kept, stays(flat_hist))


def student_kernel(requests, chunk, order, me_ref, x_ref, w_ref, s_ref, c_ref, e_ref, *refs):
    grad_refs, (gs_ref, rate_ref, part_ref) = refs[:-3], refs[-3:]
    rows, feats = x_ref.shape
    units = w_ref.shape[1]
    cand = rows // requests
    score_vec = s_ref[...].astype(F32)

    def one(r, total):
        at = pl.ds(pl.multiple_of(r * cand, cand), cand)
        preact = jnp.dot(x_ref[at, :], w_ref[...], preferred_element_type=F32)
        hidden = jnp.maximum(preact, 0.0)
        exp_scores = jnp.exp(jnp.sum(hidden * score_vec, axis=-1, keepdims=True))
        student = exp_scores / jnp.sum(exp_scores, axis=0, keepdims=True)
        live = jnp.where(preact > 0, student * score_vec, 0.0)
        part_ref[at, :] = live.astype(BF16)
        return total + jnp.sum(student * hidden, axis=0, keepdims=True)

    gs_ref[...] = lax.fori_loop(0, requests, one, jnp.zeros((1, units), F32))
    step = min(256, feats)
    held = grad_refs[0].shape[0] // chunk

    def block(i, carry):
        at = pl.ds(pl.multiple_of(i * step, step), step)
        grad = lax.dot_general(
            x_ref[:, at], part_ref[...], (((0,), (0,)), ((), ())), preferred_element_type=F32
        )
        for j in range(step // chunk):
            piece = grad[j * chunk : (j + 1) * chunk, :]
            spot = order(i * (step // chunk) + j, me_ref[0])
            for half, ref in enumerate(grad_refs):

                @pl.when(spot // held == half)
                def _(ref=ref, half=half, piece=piece, spot=spot):
                    place = jnp.clip(spot - half * held, 0, held - 1)
                    ref[pl.ds(pl.multiple_of(place * chunk, chunk), chunk), :] = piece

        return carry

    lax.fori_loop(0, feats // step, block, 0)
    rated = c_ref[...].astype(F32) * e_ref[...].astype(F32)
    focus, wide = rate_ref.shape
    gangs = ATTENDER_GANGS
    head_row = lax.broadcasted_iota(jnp.int32, (focus, wide), 0) // (focus // gangs)
    head_col = lax.broadcasted_iota(jnp.int32, (focus, wide), 1) // (wide // gangs)
    same = (head_row == head_col).astype(F32).astype(BF16)
    high = rated.astype(BF16)
    middle = (rated - high.astype(F32)).astype(BF16)
    low = (rated - high.astype(F32) - middle.astype(F32)).astype(BF16)
    rate = jnp.dot(high, same, preferred_element_type=F32)
    rate += jnp.dot(middle, same, preferred_element_type=F32)
    rate += jnp.dot(low, same, preferred_element_type=F32)
    rate_ref[...] = rate.astype(BF16)


def student_part(x, w, s, content, rating, wide, me, pieces, halves, order):
    requests, cand, feats = x.shape
    units = w.shape[1]
    rows = requests * cand
    return pl.pallas_call(
        functools.partial(student_kernel, requests, feats // pieces, order),
        out_shape=(jax.ShapeDtypeStruct((feats // halves, units), F32),) * halves
        + (
            jax.ShapeDtypeStruct((1, units), F32),
            jax.ShapeDtypeStruct((content.shape[0], wide), BF16),
        ),
        in_specs=[scalars()] + [full_vmem()] * 5,
        out_specs=(full_vmem(),) * (halves + 2),
        scratch_shapes=[VMEM((rows, units), BF16)],
        compiler_params=room(20),
        cost_estimate=pl.CostEstimate(
            flops=4 * requests * cand * feats * units, bytes_accessed=8 * 10**6, transcendentals=0
        ),
    )(me, x.reshape(rows, feats), w, s.reshape(1, units), content, rating.reshape(1, -1))


def block_scores(dims, me, payload, ask, look, rate):
    requests, hist_slots, kept, tops, gangs = dims
    focus = look.shape[0]
    span = look.shape[1] // gangs
    hist_rows, kept_rows, pieces, meta_at = rows_of(
        requests, hist_slots, kept, ask.shape[0], focus
    )
    hist = payload[:hist_rows, :]
    keys = jnp.dot(hist, look[...], preferred_element_type=F32).astype(BF16)
    values = jnp.dot(hist, rate[...], preferred_element_type=F32)
    queries = None
    for p in range(pieces):
        rows = payload[hist_rows + p * kept_rows : hist_rows + (p + 1) * kept_rows, :]
        part = jnp.dot(rows, ask[p * focus : (p + 1) * focus, :], preferred_element_type=F32)
        queries = part if queries is None else queries + part
    queries = (queries * span**-0.5).astype(BF16)
    wide = gangs * kept
    head_row = lax.broadcasted_iota(jnp.int32, (wide, look.shape[1]), 0) // kept
    head_col = lax.broadcasted_iota(jnp.int32, (wide, look.shape[1]), 1) // span
    same_head = head_row == head_col
    slot = lax.broadcasted_iota(jnp.int32, (hist_slots, wide), 0).astype(F32)
    meta = payload[meta_at : meta_at + META_ROWS, :].astype(F32)
    meta_lane = lax.broadcasted_iota(jnp.int32, meta.shape, 1)
    hit = jnp.where((meta_lane < tops) & (meta == me.astype(F32)), 1.0, 0.0)
    routed = jnp.max(hit, axis=-1, keepdims=True)
    lengths = jnp.sum(jnp.where(meta_lane == tops, meta, 0.0), axis=-1, keepdims=True)
    lane = lax.broadcasted_iota(jnp.int32, (1, kept_rows), 1) // kept
    scores = jnp.zeros((1, kept_rows), F32)
    for r in range(requests):
        q = queries[r * kept : (r + 1) * kept, :]
        q_wide = jnp.where(same_head, jnp.concatenate([q] * gangs, axis=0), jnp.zeros((), BF16))
        logits = lax.dot_general(
            keys[r * hist_slots : (r + 1) * hist_slots, :],
            q_wide,
            (((1,), (1,)), ((), ())),
            preferred_element_type=F32,
        )
        weights = jnp.where(slot < lengths[r : r + 1, :], jnp.exp(logits), 0.0)
        mixed = weights * values[r * hist_slots : (r + 1) * hist_slots, :]
        per_head = jnp.sum(mixed, axis=0, keepdims=True) / jnp.sum(weights, axis=0, keepdims=True)
        folded = per_head[:, :kept_rows]
        for b in range(1, wide // kept_rows):
            folded = folded + per_head[:, b * kept_rows : (b + 1) * kept_rows]
        shift = kept
        while shift < kept_rows:
            folded = folded + pltpu.roll(folded, shift, 1)
            shift *= 2
        scores = jnp.where((lane == r) & (routed[r : r + 1, :] > 0), folded, scores)
    return scores


def own_columns(me, rows_of_piece, sel_rows):
    focus = rows_of_piece[0].shape[1]
    own = None
    for p, rows in enumerate(rows_of_piece):
        feature = lax.broadcasted_iota(jnp.int32, (sel_rows, focus), 1) + p * focus
        wanted = lax.broadcasted_iota(jnp.int32, (sel_rows, focus), 0) + me * sel_rows
        pick = (feature == wanted).astype(F32).astype(BF16)
        got = lax.dot_general(pick, rows, (((1,), (1,)), ((), ())), preferred_element_type=F32)
        own = got if own is None else own + got
    return own.astype(BF16)


def rank_kernel(dims, sel_rows, layout, wants, first, info_ref, *refs):
    want_scores, want_hidden, parts = wants
    requests, hist_slots, kept, _, _ = dims
    n_in = sum(layout) if layout else 1
    arrays, refs = refs[:n_in], refs[n_in:]
    if want_scores:
        (a_ref, l_ref, r_ref), refs = refs[:3], refs[3:]
    if want_hidden:
        w_ref, refs = refs[0], refs[1:]
    if parts is not None:
        earlier, gs_ref, refs = refs[: len(parts)], refs[len(parts)], refs[len(parts) + 1 :]
    if want_scores:
        o_ref, refs = refs[0], refs[1:]
    if want_hidden:
        h_ref, s_ref, refs = refs[0], refs[1], refs[2:]
    buf, sems = refs
    blocks, _, focus = buf.shape
    feats = (a_ref if want_scores else w_ref).shape[0]
    hist_rows, kept_rows, pieces, _ = rows_of(requests, hist_slots, kept, feats, focus)
    low = 0 if want_scores else hist_rows
    high = low + buf.shape[1]

    def start_block(b):
        if not layout:
            fetch(arrays[0].at[b, pl.ds(low, high - low), :], buf.at[b], sems.at[b])
            return
        at, i = 0, sum(layout[:b])
        for array in arrays[i : i + layout[b]]:
            rows = array.shape[0]
            begin, end = max(at, low), min(at + rows, high)
            if begin < end:
                fetch(
                    array.at[pl.ds(begin - at, end - begin), :],
                    buf.at[b, pl.ds(begin - low, end - begin), :],
                    sems.at[b],
                )
            at += rows

    def wait_block(b):
        pltpu.make_async_copy(buf.at[b], buf.at[b], sems.at[b]).wait()

    for b in range(blocks):
        start_block(b)
    if parts is not None:
        slot = 0
        for ref, count in zip(earlier, parts):
            for b in range(count):
                o_ref[pl.ds(info_ref[1] ^ slot, 1), :] = ref[b]
                slot += 1
        scored, lanes = slot + blocks, o_ref.shape[1]
        for i in range(o_ref.shape[0] - scored):
            o_ref[scored + i : scored + i + 1, :] = gs_ref[:, i * lanes : (i + 1) * lanes]
    me = info_ref[0]
    if want_scores:

        def one(b, carry):
            wait_block(b)
            row = block_scores(dims, me, buf.at[b], a_ref, l_ref, r_ref)
            if parts is not None:
                o_ref[pl.ds(info_ref[1] ^ (first + b), 1), :] = row
            else:
                o_ref[b] = row
            return carry

        lax.fori_loop(0, blocks, one, 0)
    else:
        for b in range(blocks):
            wait_block(b)
    if want_hidden:
        rows_of_piece = []
        for p in range(pieces):
            at = hist_rows - low + p * kept_rows
            rows_of_piece.append(
                jnp.concatenate([buf[b, at : at + kept_rows, :] for b in range(blocks)], axis=0)
            )
        preact = None
        for p, rows in enumerate(rows_of_piece):
            part = jnp.dot(
                rows, w_ref[p * focus : (p + 1) * focus, :], preferred_element_type=F32
            )
            preact = part if preact is None else preact + part
        h_ref[...] = jnp.maximum(preact, 0.0).astype(BF16)
        s_ref[...] = own_columns(me, rows_of_piece, sel_rows)


def rank(dims, me, payloads, score_weights, hidden_weights, sel_rows, first=0, message=None):
    requests, _, kept, _, _ = dims
    kept_rows = requests * kept
    want_scores, want_hidden = score_weights is not None, hidden_weights is not None
    if isinstance(payloads, list):
        blocks = len(payloads)
        layout = [len(p) for p in payloads]
        arrays = [a for p in payloads for a in p]
        rows, focus = sum(a.shape[0] for a in payloads[0]), arrays[0].shape[1]
    else:
        blocks, rows, focus = payloads.shape
        layout, arrays = None, [payloads]
    if not want_scores:
        rows = kept_rows * (hidden_weights[0].shape[0] // focus)
    scratch = [VMEM((blocks, rows, focus), BF16), pltpu.SemaphoreType.DMA((blocks,))]
    weights = list(score_weights or ()) + list(hidden_weights or ())
    shapes, outs, small, parts = [], [], [], None
    if want_scores:
        if message is None:
            shapes.append(jax.ShapeDtypeStruct((blocks, 1, kept_rows), F32))
        else:
            earlier, gs = message
            parts = [e.shape[0] for e in earlier]
            small = list(earlier) + [gs]
            total = sum(parts) + blocks + gs.shape[1] // kept_rows
            shapes.append(jax.ShapeDtypeStruct((total, kept_rows), F32))
        outs.append(full_vmem())
    if want_hidden:
        units = hidden_weights[0].shape[1]
        shapes.append(jax.ShapeDtypeStruct((blocks * kept_rows, units), BF16))
        shapes.append(jax.ShapeDtypeStruct((sel_rows, blocks * kept_rows), BF16))
        outs += [full_vmem()] * 2
    flops = blocks * (7 * 10**8 * want_scores + 3 * 10**8 * want_hidden)
    return pl.pallas_call(
        functools.partial(
            rank_kernel, dims, sel_rows, layout, (want_scores, want_hidden, parts), first
        ),
        out_shape=tuple(shapes),
        in_specs=[scalars()]
        + [in_place()] * len(arrays)
        + [full_vmem()] * (len(weights) + len(small)),
        out_specs=tuple(outs),
        scratch_shapes=scratch,
        compiler_params=room(22),
        cost_estimate=pl.CostEstimate(
            flops=flops, bytes_accessed=blocks * 10**6, transcendentals=0
        ),
    )(me, *arrays, *weights, *small)


def target_kernel(kept, tops, n_parts, me_ref, got_ref, s_ref, base_ref, *refs):
    sel_refs, hid_refs = refs[:n_parts], refs[n_parts : 2 * n_parts]
    out_ref, target_ref = refs[2 * n_parts :]
    kept_rows = got_ref.shape[1]
    units = s_ref.shape[1]
    blocks = got_ref.shape[0] - units // kept_rows
    sel_rows = sel_refs[0].shape[0]
    total = got_ref[...]
    exp_teacher = jnp.exp(total[:blocks, :] / tops)
    near = lax.broadcasted_iota(jnp.int32, (kept_rows, kept_rows), 0) // kept
    far = lax.broadcasted_iota(jnp.int32, (kept_rows, kept_rows), 1) // kept
    group = (near == far).astype(F32)
    sums = jnp.dot(
        exp_teacher, group, preferred_element_type=F32, precision=lax.Precision.HIGHEST
    )
    target_ref[...] = exp_teacher / sums
    grad = jnp.zeros((sel_rows, units), F32)
    lift = jnp.zeros((1, units), F32)
    slot = 0
    for sel_ref, hid_ref in zip(sel_refs, hid_refs):
        count = sel_ref.shape[1] // kept_rows
        target = jnp.concatenate(
            [target_ref[pl.ds(me_ref[1] ^ (slot + b), 1), :] for b in range(count)], axis=1
        )
        high = target.astype(BF16).astype(F32)
        hidden = hid_ref[...]
        slot += count
        live = jnp.where(hidden > 0, jnp.ones((), BF16), jnp.zeros((), BF16))
        scaled = (sel_ref[...].astype(F32) * target).astype(BF16)
        grad += jnp.dot(scaled, live, preferred_element_type=F32)
        both = jnp.concatenate([high, target - high], axis=0).astype(BF16)
        pair = jnp.dot(both, hidden, preferred_element_type=F32)
        lift += pair[0:1, :] + pair[1:2, :]
    out_ref[:sel_rows, :] = -grad * s_ref[...].astype(F32)
    held = base_ref.shape[0]
    at = pl.ds(pl.multiple_of(me_ref[2] * held, 8), held)
    out_ref[at, :] = out_ref[at, :] + base_ref[...]
    for i in range(units // kept_rows):
        at = slice(i * kept_rows, (i + 1) * kept_rows)
        out_ref[sel_rows : sel_rows + 1, at] = total[blocks + i : blocks + i + 1, :] - lift[:, at]
    out_ref[sel_rows + 1 :, :] = jnp.zeros((out_ref.shape[0] - sel_rows - 1, units), F32)


def target_part(kept, tops, me, got, hiddens, owns, s, base):
    sel_rows = owns[0].shape[0]
    units = hiddens[0].shape[1]
    blocks = got.shape[0] - units // got.shape[1]
    parts = len(hiddens)
    return pl.pallas_call(
        functools.partial(target_kernel, kept, tops, parts),
        out_shape=jax.ShapeDtypeStruct((sel_rows + 8, units), F32),
        in_specs=[scalars()] + [full_vmem()] * (3 + 2 * parts),
        out_specs=full_vmem(),
        scratch_shapes=[VMEM((blocks, got.shape[1]), F32)],
        compiler_params=room(22),
        cost_estimate=pl.CostEstimate(flops=10**9, bytes_accessed=6 * 10**6, transcendentals=0),
    )(me, got, s.reshape(1, units), base, *owns, *hiddens)


def along(pairs):
    table = []
    for z, z_to in pairs:
        for low in range(4):
            table.append((4 * z + low, 4 * z_to + low))
    return table


def flip(bits):
    return [(i, i ^ bits) for i in range(16)]


SIBLING, Y_OVER, Z_NEAR, Z_FAR = flip(1), flip(2), flip(4), flip(8)
Z_INNER = along([(1, 2), (2, 1)])
Z_OUT = along([(1, 0), (2, 3)])


def shift(x, table, axis="shard"):
    return lax.ppermute(x, axis, table)


def gather_stages(b, me):
    inner = ((me >> 2) ^ (me >> 3)) & 1 == 1
    cut = -(-b.shape[0] // 32) * 16
    near = shift(b, Z_NEAR)
    over = shift(b, Y_OVER)
    mid = shift(b, Z_INNER)
    mid_far = shift(near, Z_INNER)
    out_far = shift(mid, Z_OUT)
    over_near = shift(near, Y_OVER)
    far = jnp.where(inner, mid_far, out_far)
    out_last = shift(mid_far, Z_OUT)
    over_far = shift(far, Y_OVER)
    last = [jnp.where(inner, mid[:cut], out_last[:cut]), jnp.where(inner, mid[cut:], out_last[cut:])]
    over_last = shift(last[0], Y_OVER)
    rest_out = shift(over_far[cut:], Z_OUT)
    rest_mid = shift(over[cut:], Z_INNER)
    over_rest = jnp.where(inner, rest_mid, rest_out)

    def both(*pieces):
        return [list(pieces), [shift(p, SIBLING) for p in pieces]]

    return [
        both(b),
        both(over) + both(near),
        both(over_near) + both(far),
        both(over_far) + both(*last),
        both(over_last, over_rest),
    ]


def halving_order(block, me):
    away = block ^ me
    z1, z0, y, core, grp = [(away >> i) & 1 for i in (4, 3, 2, 1, 0)]
    return (core << 4) | (grp << 3) | (z0 << 2) | (z1 << 1) | y


def halve(keep, sent):
    for table, axis in (
        (SIBLING, "shard"),
        ([(0, 1), (1, 0)], "group"),
        (Z_NEAR, "shard"),
        (Z_FAR, "shard"),
        (Y_OVER, "shard"),
    ):
        wide = axis == "group" or table is SIBLING
        got = shift(sent if wide else sent.astype(BF16), table, axis).astype(F32)
        half = keep.shape[0] // 2
        if table is Y_OVER:
            return keep + got
        keep, sent = keep[:half] + got[:half], keep[half:] + got[half:]


def sum_over_shard(x):
    for table in (SIBLING, Y_OVER, Z_NEAR, Z_FAR):
        x = x + shift(x, table)
    return x


def sum_kernel(a_ref, b_ref, grad_ref, score_ref):
    rows = grad_ref.shape[0]
    grad_ref[...] = a_ref[:rows, :] + b_ref[:rows, :]
    score_ref[...] = a_ref[rows : rows + 1, :] + b_ref[rows : rows + 1, :]


def sum_two(a, b, rows):
    return pl.pallas_call(
        sum_kernel,
        out_shape=(
            jax.ShapeDtypeStruct((rows, a.shape[1]), F32),
            jax.ShapeDtypeStruct((1, a.shape[1]), F32),
        ),
        in_specs=[full_vmem()] * 2,
        out_specs=(full_vmem(),) * 2,
        compiler_params=room(4),
    )(a, b)


def body(
    offer_attribute_matrix,
    kept_offers,
    expert_target,
    sequence_extent,
    behaviour_sequence,
    inner_projection_matrix,
    student_rating_vector,
    asking_matrix,
    lookup_matrix,
    content_matrix,
    expert_rating_vector,
):
    requests, _, feats = offer_attribute_matrix.shape
    kept = kept_offers.shape[1]
    hist_slots, _ = behaviour_sequence.shape[1:]
    tops = expert_target.shape[1]
    units = inner_projection_matrix.shape[1]
    n_shard = lax.axis_size("shard")
    sel_rows = feats // n_shard
    me = lax.axis_index("shard")
    n_group = lax.axis_size("group")
    grp = lax.axis_index("group")

    payload = pack(
        offer_attribute_matrix, kept_offers, behaviour_sequence, expert_target, sequence_extent
    )
    linked = n_shard == 16 and n_group == 2
    place = (me * n_group + grp if linked else me).astype(jnp.int32).reshape(1)
    stack = (
        offer_attribute_matrix,
        inner_projection_matrix,
        student_rating_vector,
        content_matrix[0],
        expert_rating_vector[0],
        ATTENDER_GANGS * kept,
        place,
    )
    if linked:
        stages = gather_stages(payload, me)
        keep, sent, gs_student, rate = student_part(
            *stack, n_shard * n_group, 2, halving_order
        )
        base = halve(keep, sent)
        info = jnp.stack([me, me, grp]).astype(jnp.int32)
    else:
        payloads = lax.all_gather(payload, "shard", axis=0, tiled=False)
        stages = [payloads[b : b + 4] for b in range(0, n_shard, 4)]
        grad_student, gs_student, rate = student_part(
            *stack, n_shard, 1, lambda block, at: block
        )
        base = lax.psum_scatter(grad_student, "shard", scatter_dimension=0, tiled=True)
        info = jnp.stack([me, 0 * me, 0 * me]).astype(jnp.int32)

    dims = (requests, hist_slots, kept, tops, ATTENDER_GANGS)
    score_weights = (asking_matrix[0], lookup_matrix[0], rate)
    hidden_weights = (inner_projection_matrix,)
    scores, hiddens, owns = [], [], []
    late = len(stages) - 2 if linked else len(stages) - 1
    for number, stage in enumerate(stages[:-1]):
        if number < late:
            score, hidden, own = rank(dims, info, stage, score_weights, hidden_weights, sel_rows)
            hiddens.append(hidden)
            owns.append(own)
        else:
            (score,) = rank(dims, info, stage, score_weights, None, sel_rows)
        scores.append(score)
    known = sum(s.shape[0] for s in scores)
    (send,) = rank(
        dims, info, stages[-1], score_weights, None, sel_rows, known, (scores, gs_student)
    )
    rest = stages[-2] + stages[-1] if linked else stages[-1]
    hidden, own = rank(dims, info, rest, None, hidden_weights, sel_rows)
    hiddens.append(hidden)
    owns.append(own)
    got = sum_over_shard(send) if linked else lax.psum(send, "shard")
    mine = target_part(kept, tops, info, got, hiddens, owns, student_rating_vector, base)
    if linked:
        grad, lift = sum_two(mine, shift(mine, [(0, 1), (1, 0)], "group"), sel_rows)
        return grad, lift.reshape(units)
    whole = lax.psum(mine, "group")
    return whole[:sel_rows], whole[sel_rows]


def solution(mesh):
    placed = (
        P(("group", "shard"), None, None),
        P(("group", "shard"), None),
        P(("group", "shard"), None),
        P(("group", "shard")),
        P(("group", "shard"), None, None),
        P(),
        P(),
        P("shard", None, None),
        P("shard", None, None),
        P("shard", None, None),
        P("shard", None),
    )
    return jax.shard_map(
        body, mesh=mesh, in_specs=placed, out_specs=(P("shard", None), P()), check_vma=False
    )
```

```python
import functools

import jax
import jax.numpy as jnp
from jax import lax
from jax.experimental import pallas as pl
from jax.experimental.pallas import tpu as pltpu
from jax.sharding import PartitionSpec as P


ATTENDER_GANGS = 8
META_ROWS = 16
VMEM = pltpu.VMEM
F32 = jnp.float32
BF16 = jnp.bfloat16


def full_vmem():
    return pl.BlockSpec(memory_space=pltpu.VMEM)


def in_place():
    return pl.BlockSpec(memory_space=pl.ANY)


def scalars():
    return pl.BlockSpec(memory_space=pltpu.SMEM)


def room(mib):
    return pltpu.CompilerParams(vmem_limit_bytes=mib * 2**20)


def stays(x):
    return pltpu.with_memory_space_constraint(x, pltpu.HBM)


def fetch(source, target, sem):
    copy = pltpu.make_async_copy(source, target, sem)
    copy.start()
    return copy.wait


def rows_of(requests, hist_slots, kept, feature_span, focus_span):
    hist_rows = requests * hist_slots
    kept_rows = requests * kept
    pieces = feature_span // focus_span
    return hist_rows, kept_rows, pieces, hist_rows + kept_rows * pieces


def pack_kernel(target_ref, extent_ref, x_hbm, kept_ref, hist_hbm, out_ref, x_ref, sems):
    requests, cand, _ = x_ref.shape
    kept = kept_ref.shape[1]
    focus = hist_hbm.shape[1]
    hist_rows = hist_hbm.shape[0]
    tops = target_ref.shape[1]
    pieces = x_ref.shape[2] // focus
    meta_at = hist_rows + pieces * requests * kept
    waits = [fetch(x_hbm.at[r], x_ref.at[r], sems.at[r]) for r in range(requests)]
    wait_hist = fetch(hist_hbm, out_ref.at[pl.ds(0, hist_rows), :], sems.at[requests])
    row = lax.broadcasted_iota(jnp.int32, (META_ROWS, focus), 0)
    lane = lax.broadcasted_iota(jnp.int32, (META_ROWS, focus), 1)
    meta = jnp.zeros((META_ROWS, focus), jnp.int32)
    for r in range(requests):
        for t in range(tops):
            meta = jnp.where((row == r) & (lane == t), target_ref[r, t], meta)
        meta = jnp.where((row == r) & (lane == tops), extent_ref[r], meta)
    out_ref[meta_at:, :] = meta.astype(F32).astype(BF16)
    for r in range(requests):
        waits[r]()
        cand_of = lax.broadcasted_iota(jnp.int32, (cand, kept), 0)
        pick = (cand_of == kept_ref[r : r + 1, :]).astype(F32).astype(BF16)
        for p in range(pieces):
            rows = lax.dot_general(
                pick,
                x_ref[r, :, p * focus : (p + 1) * focus],
                (((0,), (0,)), ((), ())),
                preferred_element_type=F32,
            )
            at = hist_rows + p * requests * kept + r * kept
            out_ref[at : at + kept, :] = rows.astype(BF16)
    wait_hist()


def pack(x, kept, hist, targets, extents):
    requests, _, feats = x.shape
    focus = hist.shape[2]
    flat_hist = hist.reshape(-1, focus)
    total = rows_of(requests, hist.shape[1], kept.shape[1], feats, focus)[3] + META_ROWS
    return pl.pallas_call(
        pack_kernel,
        out_shape=jax.ShapeDtypeStruct((total, focus), BF16),
        in_specs=[scalars(), scalars(), in_place(), full_vmem(), in_place()],
        out_specs=full_vmem(),
        scratch_shapes=[VMEM(x.shape, BF16), pltpu.SemaphoreType.DMA((requests + 1,))],
        cost_estimate=pl.CostEstimate(flops=10**8, bytes_accessed=3 * 10**6, transcendentals=0),
    )(targets, extents, stays(x), stays(kept), stays(flat_hist))


def student_kernel(requests, chunk, order, me_ref, x_ref, w_ref, s_ref, c_ref, e_ref, *refs):
    grad_refs, (gs_ref, rate_ref, part_ref) = refs[:-3], refs[-3:]
    rows, feats = x_ref.shape
    units = w_ref.shape[1]
    cand = rows // requests
    score_vec = s_ref[...].astype(F32)

    def one(r, total):
        at = pl.ds(pl.multiple_of(r * cand, cand), cand)
        preact = jnp.dot(x_ref[at, :], w_ref[...], preferred_element_type=F32)
        hidden = jnp.maximum(preact, 0.0)
        exp_scores = jnp.exp(jnp.sum(hidden * score_vec, axis=-1, keepdims=True))
        student = exp_scores / jnp.sum(exp_scores, axis=0, keepdims=True)
        live = jnp.where(preact > 0, student * score_vec, 0.0)
        part_ref[at, :] = live.astype(BF16)
        return total + jnp.sum(student * hidden, axis=0, keepdims=True)

    gs_ref[...] = lax.fori_loop(0, requests, one, jnp.zeros((1, units), F32))
    step = min(256, feats)
    held = grad_refs[0].shape[0] // chunk

    def block(i, carry):
        at = pl.ds(pl.multiple_of(i * step, step), step)
        grad = lax.dot_general(
            x_ref[:, at], part_ref[...], (((0,), (0,)), ((), ())), preferred_element_type=F32
        )
        for j in range(step // chunk):
            piece = grad[j * chunk : (j + 1) * chunk, :]
            spot = order(i * (step // chunk) + j, me_ref[0])
            for half, ref in enumerate(grad_refs):

                @pl.when(spot // held == half)
                def _(ref=ref, half=half, piece=piece, spot=spot):
                    place = jnp.clip(spot - half * held, 0, held - 1)
                    ref[pl.ds(pl.multiple_of(place * chunk, chunk), chunk), :] = piece

        return carry

    lax.fori_loop(0, feats // step, block, 0)
    rated = c_ref[...].astype(F32) * e_ref[...].astype(F32)
    focus, wide = rate_ref.shape
    gangs = ATTENDER_GANGS
    head_row = lax.broadcasted_iota(jnp.int32, (focus, wide), 0) // (focus // gangs)
    head_col = lax.broadcasted_iota(jnp.int32, (focus, wide), 1) // (wide // gangs)
    same = (head_row == head_col).astype(F32).astype(BF16)
    high = rated.astype(BF16)
    middle = (rated - high.astype(F32)).astype(BF16)
    low = (rated - high.astype(F32) - middle.astype(F32)).astype(BF16)
    rate = jnp.dot(high, same, preferred_element_type=F32)
    rate += jnp.dot(middle, same, preferred_element_type=F32)
    rate += jnp.dot(low, same, preferred_element_type=F32)
    rate_ref[...] = rate.astype(BF16)


def student_part(x, w, s, content, rating, wide, me, pieces, halves, order):
    requests, cand, feats = x.shape
    units = w.shape[1]
    rows = requests * cand
    return pl.pallas_call(
        functools.partial(student_kernel, requests, feats // pieces, order),
        out_shape=(jax.ShapeDtypeStruct((feats // halves, units), F32),) * halves
        + (
            jax.ShapeDtypeStruct((1, units), F32),
            jax.ShapeDtypeStruct((content.shape[0], wide), BF16),
        ),
        in_specs=[scalars()] + [full_vmem()] * 5,
        out_specs=(full_vmem(),) * (halves + 2),
        scratch_shapes=[VMEM((rows, units), BF16)],
        compiler_params=room(20),
        cost_estimate=pl.CostEstimate(
            flops=4 * requests * cand * feats * units, bytes_accessed=8 * 10**6, transcendentals=0
        ),
    )(me, x.reshape(rows, feats), w, s.reshape(1, units), content, rating.reshape(1, -1))


def block_scores(dims, me, payload, ask, look, rate):
    requests, hist_slots, kept, tops, gangs = dims
    focus = look.shape[0]
    span = look.shape[1] // gangs
    hist_rows, kept_rows, pieces, meta_at = rows_of(
        requests, hist_slots, kept, ask.shape[0], focus
    )
    hist = payload[:hist_rows, :]
    keys = jnp.dot(hist, look[...], preferred_element_type=F32).astype(BF16)
    values = jnp.dot(hist, rate[...], preferred_element_type=F32)
    queries = None
    for p in range(pieces):
        rows = payload[hist_rows + p * kept_rows : hist_rows + (p + 1) * kept_rows, :]
        part = jnp.dot(rows, ask[p * focus : (p + 1) * focus, :], preferred_element_type=F32)
        queries = part if queries is None else queries + part
    queries = (queries * span**-0.5).astype(BF16)
    wide = gangs * kept
    head_row = lax.broadcasted_iota(jnp.int32, (wide, look.shape[1]), 0) // kept
    head_col = lax.broadcasted_iota(jnp.int32, (wide, look.shape[1]), 1) // span
    same_head = head_row == head_col
    slot = lax.broadcasted_iota(jnp.int32, (hist_slots, wide), 0).astype(F32)
    meta = payload[meta_at : meta_at + META_ROWS, :].astype(F32)
    meta_lane = lax.broadcasted_iota(jnp.int32, meta.shape, 1)
    hit = jnp.where((meta_lane < tops) & (meta == me.astype(F32)), 1.0, 0.0)
    routed = jnp.max(hit, axis=-1, keepdims=True)
    lengths = jnp.sum(jnp.where(meta_lane == tops, meta, 0.0), axis=-1, keepdims=True)
    lane = lax.broadcasted_iota(jnp.int32, (1, kept_rows), 1) // kept
    scores = jnp.zeros((1, kept_rows), F32)
    for r in range(requests):
        q = queries[r * kept : (r + 1) * kept, :]
        q_wide = jnp.where(same_head, jnp.concatenate([q] * gangs, axis=0), jnp.zeros((), BF16))
        logits = lax.dot_general(
            keys[r * hist_slots : (r + 1) * hist_slots, :],
            q_wide,
            (((1,), (1,)), ((), ())),
            preferred_element_type=F32,
        )
        weights = jnp.where(slot < lengths[r : r + 1, :], jnp.exp(logits), 0.0)
        mixed = weights * values[r * hist_slots : (r + 1) * hist_slots, :]
        per_head = jnp.sum(mixed, axis=0, keepdims=True) / jnp.sum(weights, axis=0, keepdims=True)
        folded = per_head[:, :kept_rows]
        for b in range(1, wide // kept_rows):
            folded = folded + per_head[:, b * kept_rows : (b + 1) * kept_rows]
        shift = kept
        while shift < kept_rows:
            folded = folded + pltpu.roll(folded, shift, 1)
            shift *= 2
        scores = jnp.where((lane == r) & (routed[r : r + 1, :] > 0), folded, scores)
    return scores


def own_columns(me, rows_of_piece, sel_rows):
    focus = rows_of_piece[0].shape[1]
    own = None
    for p, rows in enumerate(rows_of_piece):
        feature = lax.broadcasted_iota(jnp.int32, (sel_rows, focus), 1) + p * focus
        wanted = lax.broadcasted_iota(jnp.int32, (sel_rows, focus), 0) + me * sel_rows
        pick = (feature == wanted).astype(F32).astype(BF16)
        got = lax.dot_general(pick, rows, (((1,), (1,)), ((), ())), preferred_element_type=F32)
        own = got if own is None else own + got
    return own.astype(BF16)


def rank_kernel(dims, sel_rows, layout, wants, first, info_ref, *refs):
    want_scores, want_hidden, parts = wants
    requests, hist_slots, kept, _, _ = dims
    n_in = sum(layout) if layout else 1
    arrays, refs = refs[:n_in], refs[n_in:]
    if want_scores:
        (a_ref, l_ref, r_ref), refs = refs[:3], refs[3:]
    if want_hidden:
        w_ref, refs = refs[0], refs[1:]
    if parts is not None:
        earlier, gs_ref, refs = refs[: len(parts)], refs[len(parts)], refs[len(parts) + 1 :]
    if want_scores:
        o_ref, refs = refs[0], refs[1:]
    if want_hidden:
        h_ref, s_ref, refs = refs[0], refs[1], refs[2:]
    buf, sems = refs
    blocks, _, focus = buf.shape
    feats = (a_ref if want_scores else w_ref).shape[0]
    hist_rows, kept_rows, pieces, _ = rows_of(requests, hist_slots, kept, feats, focus)
    low = 0 if want_scores else hist_rows
    high = low + buf.shape[1]

    def start_block(b):
        if not layout:
            fetch(arrays[0].at[b, pl.ds(low, high - low), :], buf.at[b], sems.at[b])
            return
        at, i = 0, sum(layout[:b])
        for array in arrays[i : i + layout[b]]:
            rows = array.shape[0]
            begin, end = max(at, low), min(at + rows, high)
            if begin < end:
                fetch(
                    array.at[pl.ds(begin - at, end - begin), :],
                    buf.at[b, pl.ds(begin - low, end - begin), :],
                    sems.at[b],
                )
            at += rows

    def wait_block(b):
        pltpu.make_async_copy(buf.at[b], buf.at[b], sems.at[b]).wait()

    for b in range(blocks):
        start_block(b)
    if parts is not None:
        slot = 0
        for ref, count in zip(earlier, parts):
            for b in range(count):
                o_ref[pl.ds(info_ref[1] ^ slot, 1), :] = ref[b]
                slot += 1
        scored, lanes = slot + blocks, o_ref.shape[1]
        for i in range(o_ref.shape[0] - scored):
            o_ref[scored + i : scored + i + 1, :] = gs_ref[:, i * lanes : (i + 1) * lanes]
    me = info_ref[0]
    if want_scores:

        def one(b, carry):
            wait_block(b)
            row = block_scores(dims, me, buf.at[b], a_ref, l_ref, r_ref)
            if parts is not None:
                o_ref[pl.ds(info_ref[1] ^ (first + b), 1), :] = row
            else:
                o_ref[b] = row
            return carry

        lax.fori_loop(0, blocks, one, 0)
    else:
        for b in range(blocks):
            wait_block(b)
    if want_hidden:
        rows_of_piece = []
        for p in range(pieces):
            at = hist_rows - low + p * kept_rows
            rows_of_piece.append(
                jnp.concatenate([buf[b, at : at + kept_rows, :] for b in range(blocks)], axis=0)
            )
        preact = None
        for p, rows in enumerate(rows_of_piece):
            part = jnp.dot(
                rows, w_ref[p * focus : (p + 1) * focus, :], preferred_element_type=F32
            )
            preact = part if preact is None else preact + part
        h_ref[...] = jnp.maximum(preact, 0.0).astype(BF16)
        s_ref[...] = own_columns(me, rows_of_piece, sel_rows)


def rank(dims, me, payloads, score_weights, hidden_weights, sel_rows, first=0, message=None):
    requests, _, kept, _, _ = dims
    kept_rows = requests * kept
    want_scores, want_hidden = score_weights is not None, hidden_weights is not None
    if isinstance(payloads, list):
        blocks = len(payloads)
        layout = [len(p) for p in payloads]
        arrays = [a for p in payloads for a in p]
        rows, focus = sum(a.shape[0] for a in payloads[0]), arrays[0].shape[1]
    else:
        blocks, rows, focus = payloads.shape
        layout, arrays = None, [payloads]
    if not want_scores:
        rows = kept_rows * (hidden_weights[0].shape[0] // focus)
    scratch = [VMEM((blocks, rows, focus), BF16), pltpu.SemaphoreType.DMA((blocks,))]
    weights = list(score_weights or ()) + list(hidden_weights or ())
    shapes, outs, small, parts = [], [], [], None
    if want_scores:
        if message is None:
            shapes.append(jax.ShapeDtypeStruct((blocks, 1, kept_rows), F32))
        else:
            earlier, gs = message
            parts = [e.shape[0] for e in earlier]
            small = list(earlier) + [gs]
            total = sum(parts) + blocks + gs.shape[1] // kept_rows
            shapes.append(jax.ShapeDtypeStruct((total, kept_rows), F32))
        outs.append(full_vmem())
    if want_hidden:
        units = hidden_weights[0].shape[1]
        shapes.append(jax.ShapeDtypeStruct((blocks * kept_rows, units), BF16))
        shapes.append(jax.ShapeDtypeStruct((sel_rows, blocks * kept_rows), BF16))
        outs += [full_vmem()] * 2
    flops = blocks * (7 * 10**8 * want_scores + 3 * 10**8 * want_hidden)
    return pl.pallas_call(
        functools.partial(
            rank_kernel, dims, sel_rows, layout, (want_scores, want_hidden, parts), first
        ),
        out_shape=tuple(shapes),
        in_specs=[scalars()]
        + [in_place()] * len(arrays)
        + [full_vmem()] * (len(weights) + len(small)),
        out_specs=tuple(outs),
        scratch_shapes=scratch,
        compiler_params=room(22),
        cost_estimate=pl.CostEstimate(
            flops=flops, bytes_accessed=blocks * 10**6, transcendentals=0
        ),
    )(me, *arrays, *weights, *small)


def target_kernel(kept, tops, n_parts, me_ref, got_ref, s_ref, base_ref, *refs):
    sel_refs, hid_refs = refs[:n_parts], refs[n_parts : 2 * n_parts]
    out_ref, short_ref, target_ref = refs[2 * n_parts :]
    kept_rows = got_ref.shape[1]
    units = s_ref.shape[1]
    blocks = got_ref.shape[0] - units // kept_rows
    sel_rows = sel_refs[0].shape[0]
    total = got_ref[...]
    exp_teacher = jnp.exp(total[:blocks, :] / tops)
    near = lax.broadcasted_iota(jnp.int32, (kept_rows, kept_rows), 0) // kept
    far = lax.broadcasted_iota(jnp.int32, (kept_rows, kept_rows), 1) // kept
    group = (near == far).astype(F32)
    sums = jnp.dot(
        exp_teacher, group, preferred_element_type=F32, precision=lax.Precision.HIGHEST
    )
    target_ref[...] = exp_teacher / sums
    grad = jnp.zeros((sel_rows, units), F32)
    lift = jnp.zeros((1, units), F32)
    slot = 0
    for sel_ref, hid_ref in zip(sel_refs, hid_refs):
        count = sel_ref.shape[1] // kept_rows
        target = jnp.concatenate(
            [target_ref[pl.ds(me_ref[1] ^ (slot + b), 1), :] for b in range(count)], axis=1
        )
        high = target.astype(BF16).astype(F32)
        hidden = hid_ref[...]
        slot += count
        live = jnp.where(hidden > 0, jnp.ones((), BF16), jnp.zeros((), BF16))
        scaled = sel_ref[...].astype(F32) * target
        upper = scaled.astype(BF16)
        lower = (scaled - upper.astype(F32)).astype(BF16)
        halves = jnp.dot(
            jnp.concatenate([upper, lower], axis=0), live, preferred_element_type=F32
        )
        grad += halves[:sel_rows, :] + halves[sel_rows:, :]
        both = jnp.concatenate([high, target - high], axis=0).astype(BF16)
        pair = jnp.dot(both, hidden, preferred_element_type=F32)
        lift += pair[0:1, :] + pair[1:2, :]
    out_ref[:sel_rows, :] = -grad * s_ref[...].astype(F32)
    held = base_ref.shape[0]
    at = pl.ds(pl.multiple_of(me_ref[2] * held, 8), held)
    out_ref[at, :] = out_ref[at, :] + base_ref[...]
    for i in range(units // kept_rows):
        at = slice(i * kept_rows, (i + 1) * kept_rows)
        out_ref[sel_rows : sel_rows + 1, at] = total[blocks + i : blocks + i + 1, :] - lift[:, at]
    out_ref[sel_rows + 1 :, :] = jnp.zeros((out_ref.shape[0] - sel_rows - 1, units), F32)
    row = out_ref[sel_rows : sel_rows + 1, :]
    short_ref[...] = out_ref[...].astype(BF16)
    short_ref[sel_rows + 1 : sel_rows + 2, :] = (row - row.astype(BF16).astype(F32)).astype(BF16)


def target_part(kept, tops, me, got, hiddens, owns, s, base):
    sel_rows = owns[0].shape[0]
    units = hiddens[0].shape[1]
    blocks = got.shape[0] - units // got.shape[1]
    parts = len(hiddens)
    return pl.pallas_call(
        functools.partial(target_kernel, kept, tops, parts),
        out_shape=tuple(jax.ShapeDtypeStruct((sel_rows + 16, units), t) for t in (F32, BF16)),
        in_specs=[scalars()] + [full_vmem()] * (3 + 2 * parts),
        out_specs=(full_vmem(),) * 2,
        scratch_shapes=[VMEM((blocks, got.shape[1]), F32)],
        compiler_params=room(22),
        cost_estimate=pl.CostEstimate(flops=10**9, bytes_accessed=6 * 10**6, transcendentals=0),
    )(me, got, s.reshape(1, units), base, *owns, *hiddens)


def along(pairs):
    table = []
    for z, z_to in pairs:
        for low in range(4):
            table.append((4 * z + low, 4 * z_to + low))
    return table


def flip(bits):
    return [(i, i ^ bits) for i in range(16)]


SIBLING, Y_OVER, Z_NEAR, Z_FAR = flip(1), flip(2), flip(4), flip(8)
Z_INNER = along([(1, 2), (2, 1)])
Z_OUT = along([(1, 0), (2, 3)])


def shift(x, table, axis="shard"):
    return lax.ppermute(x, axis, table)


def gather_stages(b, me):
    inner = ((me >> 2) ^ (me >> 3)) & 1 == 1
    cut = -(-b.shape[0] // 32) * 16
    near = shift(b, Z_NEAR)
    over = shift(b, Y_OVER)
    mid = shift(b, Z_INNER)
    mid_far = shift(near, Z_INNER)
    out_far = shift(mid, Z_OUT)
    over_near = shift(near, Y_OVER)
    far = jnp.where(inner, mid_far, out_far)
    out_last = shift(mid_far, Z_OUT)
    over_far = shift(far, Y_OVER)
    last = [jnp.where(inner, mid[:cut], out_last[:cut]), jnp.where(inner, mid[cut:], out_last[cut:])]
    over_last = shift(last[0], Y_OVER)
    rest_out = shift(over_far[cut:], Z_OUT)
    rest_mid = shift(over[cut:], Z_INNER)
    over_rest = jnp.where(inner, rest_mid, rest_out)

    def both(*pieces):
        return [list(pieces), [shift(p, SIBLING) for p in pieces]]

    return [
        both(b) + both(over) + both(near),
        both(over_near) + both(far),
        both(over_far) + both(*last),
        both(over_last, over_rest),
    ]


def halving_order(block, me):
    away = block ^ me
    z1, z0, y, core, grp = [(away >> i) & 1 for i in (4, 3, 2, 1, 0)]
    return (core << 4) | (grp << 3) | (z0 << 2) | (z1 << 1) | y


def halve(keep, sent):
    for table, axis in (
        (SIBLING, "shard"),
        ([(0, 1), (1, 0)], "group"),
        (Z_NEAR, "shard"),
        (Z_FAR, "shard"),
        (Y_OVER, "shard"),
    ):
        wide = axis == "group" or table is SIBLING
        got = shift(sent if wide else sent.astype(BF16), table, axis).astype(F32)
        half = keep.shape[0] // 2
        if table is Y_OVER:
            return keep + got
        keep, sent = keep[:half] + got[:half], keep[half:] + got[half:]


def sum_over_shard(x):
    for table in (SIBLING, Y_OVER, Z_NEAR, Z_FAR):
        x = x + shift(x, table)
    return x


def sum_kernel(a_ref, b_ref, grad_ref, score_ref):
    rows = grad_ref.shape[0]
    grad_ref[...] = a_ref[:rows, :] + b_ref[:rows, :].astype(F32)
    pair = b_ref[rows : rows + 2, :].astype(F32)
    score_ref[...] = a_ref[rows : rows + 1, :] + (pair[0:1, :] + pair[1:2, :])


def sum_two(a, b, rows):
    return pl.pallas_call(
        sum_kernel,
        out_shape=(
            jax.ShapeDtypeStruct((rows, a.shape[1]), F32),
            jax.ShapeDtypeStruct((1, a.shape[1]), F32),
        ),
        in_specs=[full_vmem()] * 2,
        out_specs=(full_vmem(),) * 2,
        compiler_params=room(4),
    )(a, b)


def body(
    offer_attribute_matrix,
    kept_offers,
    expert_target,
    sequence_extent,
    behaviour_sequence,
    inner_projection_matrix,
    student_rating_vector,
    asking_matrix,
    lookup_matrix,
    content_matrix,
    expert_rating_vector,
):
    requests, _, feats = offer_attribute_matrix.shape
    kept = kept_offers.shape[1]
    hist_slots, _ = behaviour_sequence.shape[1:]
    tops = expert_target.shape[1]
    units = inner_projection_matrix.shape[1]
    n_shard = lax.axis_size("shard")
    sel_rows = feats // n_shard
    me = lax.axis_index("shard")
    n_group = lax.axis_size("group")
    grp = lax.axis_index("group")

    payload = pack(
        offer_attribute_matrix, kept_offers, behaviour_sequence, expert_target, sequence_extent
    )
    linked = n_shard == 16 and n_group == 2
    place = (me * n_group + grp if linked else me).astype(jnp.int32).reshape(1)
    stack = (
        offer_attribute_matrix,
        inner_projection_matrix,
        student_rating_vector,
        content_matrix[0],
        expert_rating_vector[0],
        ATTENDER_GANGS * kept,
        place,
    )
    if linked:
        stages = gather_stages(payload, me)
        keep, sent, gs_student, rate = student_part(
            *stack, n_shard * n_group, 2, halving_order
        )
        base = halve(keep, sent)
        info = jnp.stack([me, me, grp]).astype(jnp.int32)
    else:
        payloads = lax.all_gather(payload, "shard", axis=0, tiled=False)
        stages = [payloads[b : b + 4] for b in range(0, n_shard, 4)]
        grad_student, gs_student, rate = student_part(
            *stack, n_shard, 1, lambda block, at: block
        )
        base = lax.psum_scatter(grad_student, "shard", scatter_dimension=0, tiled=True)
        info = jnp.stack([me, 0 * me, 0 * me]).astype(jnp.int32)

    dims = (requests, hist_slots, kept, tops, ATTENDER_GANGS)
    score_weights = (asking_matrix[0], lookup_matrix[0], rate)
    hidden_weights = (inner_projection_matrix,)
    scores, hiddens, owns = [], [], []
    late = len(stages) - 2 if linked else len(stages) - 1
    for number, stage in enumerate(stages[:-1]):
        if number < late:
            score, hidden, own = rank(dims, info, stage, score_weights, hidden_weights, sel_rows)
            hiddens.append(hidden)
            owns.append(own)
        else:
            (score,) = rank(dims, info, stage, score_weights, None, sel_rows)
        scores.append(score)
    known = sum(s.shape[0] for s in scores)
    (send,) = rank(
        dims, info, stages[-1], score_weights, None, sel_rows, known, (scores, gs_student)
    )
    rest = stages[-2] + stages[-1] if linked else stages[-1]
    hidden, own = rank(dims, info, rest, None, hidden_weights, sel_rows)
    hiddens.append(hidden)
    owns.append(own)
    got = sum_over_shard(send) if linked else lax.psum(send, "shard")
    mine, short = target_part(kept, tops, info, got, hiddens, owns, student_rating_vector, base)
    if linked:
        grad, lift = sum_two(mine, shift(short, [(0, 1), (1, 0)], "group"), sel_rows)
        return grad, lift.reshape(units)
    whole = lax.psum(mine, "group")
    return whole[:sel_rows], whole[sel_rows]


def solution(mesh):
    placed = (
        P(("group", "shard"), None, None),
        P(("group", "shard"), None),
        P(("group", "shard"), None),
        P(("group", "shard")),
        P(("group", "shard"), None, None),
        P(),
        P(),
        P("shard", None, None),
        P("shard", None, None),
        P("shard", None, None),
        P("shard", None),
    )
    return jax.shard_map(
        body, mesh=mesh, in_specs=placed, out_specs=(P("shard", None), P()), check_vma=False
    )
```

```python
import functools

import jax
import jax.numpy as jnp
from jax import lax
from jax.experimental import pallas as pl
from jax.experimental.pallas import tpu as pltpu
from jax.sharding import PartitionSpec as P


ATTENDER_GANGS = 8
META_ROWS = 16
VMEM = pltpu.VMEM
F32 = jnp.float32
BF16 = jnp.bfloat16


def full_vmem():
    return pl.BlockSpec(memory_space=pltpu.VMEM)


def in_place():
    return pl.BlockSpec(memory_space=pl.ANY)


def scalars():
    return pl.BlockSpec(memory_space=pltpu.SMEM)


def room(mib):
    return pltpu.CompilerParams(vmem_limit_bytes=mib * 2**20)


def stays(x):
    return pltpu.with_memory_space_constraint(x, pltpu.HBM)


def fetch(source, target, sem):
    copy = pltpu.make_async_copy(source, target, sem)
    copy.start()
    return copy.wait


def rows_of(requests, hist_slots, kept, feature_span, focus_span):
    hist_rows = requests * hist_slots
    kept_rows = requests * kept
    pieces = feature_span // focus_span
    return hist_rows, kept_rows, pieces, hist_rows + kept_rows * pieces


def pack_kernel(
    target_ref, extent_ref, x_hbm, kept_ref, hist_hbm, out_hbm, x_ref, out_ref, sems
):
    requests, cand, _ = x_ref.shape
    kept = kept_ref.shape[1]
    focus = hist_hbm.shape[1]
    hist_rows = hist_hbm.shape[0]
    tops = target_ref.shape[1]
    pieces = x_ref.shape[2] // focus
    meta_at = hist_rows + pieces * requests * kept
    wait_hist = fetch(hist_hbm, out_ref.at[pl.ds(0, hist_rows), :], sems.at[requests])
    waits = [fetch(x_hbm.at[r], x_ref.at[r], sems.at[r]) for r in range(requests)]
    row = lax.broadcasted_iota(jnp.int32, (META_ROWS, focus), 0)
    lane = lax.broadcasted_iota(jnp.int32, (META_ROWS, focus), 1)
    meta = jnp.zeros((META_ROWS, focus), jnp.int32)
    for r in range(requests):
        for t in range(tops):
            meta = jnp.where((row == r) & (lane == t), target_ref[r, t], meta)
        meta = jnp.where((row == r) & (lane == tops), extent_ref[r], meta)
    out_ref[meta_at:, :] = meta.astype(F32).astype(BF16)
    wait_hist()
    at = pl.ds(0, hist_rows)
    wait_out = fetch(out_ref.at[at, :], out_hbm.at[at, :], sems.at[requests])
    for r in range(requests):
        waits[r]()
        cand_of = lax.broadcasted_iota(jnp.int32, (cand, kept), 0)
        pick = (cand_of == kept_ref[r : r + 1, :]).astype(F32).astype(BF16)
        for p in range(pieces):
            rows = lax.dot_general(
                pick,
                x_ref[r, :, p * focus : (p + 1) * focus],
                (((0,), (0,)), ((), ())),
                preferred_element_type=F32,
            )
            at = hist_rows + p * requests * kept + r * kept
            out_ref[at : at + kept, :] = rows.astype(BF16)
    at = pl.ds(hist_rows, out_ref.shape[0] - hist_rows)
    wait_rest = fetch(out_ref.at[at, :], out_hbm.at[at, :], sems.at[0])
    wait_out()
    wait_rest()


def pack(x, kept, hist, targets, extents):
    requests, _, feats = x.shape
    focus = hist.shape[2]
    flat_hist = hist.reshape(-1, focus)
    total = rows_of(requests, hist.shape[1], kept.shape[1], feats, focus)[3] + META_ROWS
    return pl.pallas_call(
        pack_kernel,
        out_shape=jax.ShapeDtypeStruct((total, focus), BF16),
        in_specs=[scalars(), scalars(), in_place(), full_vmem(), in_place()],
        out_specs=in_place(),
        scratch_shapes=[
            VMEM(x.shape, BF16),
            VMEM((total, focus), BF16),
            pltpu.SemaphoreType.DMA((requests + 1,)),
        ],
        cost_estimate=pl.CostEstimate(flops=10**8, bytes_accessed=3 * 10**6, transcendentals=0),
    )(targets, extents, stays(x), stays(kept), stays(flat_hist))


def student_kernel(requests, chunk, order, me_ref, x_ref, w_ref, s_ref, c_ref, e_ref, *refs):
    grad_refs, (gs_ref, rate_ref, part_ref, less_ref) = refs[:-4], refs[-4:]
    rows, feats = x_ref.shape
    units = w_ref.shape[1]
    cand = rows // requests
    score_vec = s_ref[...].astype(F32)

    def one(r, total):
        at = pl.ds(pl.multiple_of(r * cand, cand), cand)
        preact = jnp.dot(x_ref[at, :], w_ref[...], preferred_element_type=F32)
        hidden = jnp.maximum(preact, 0.0)
        exp_scores = jnp.exp(jnp.sum(hidden * score_vec, axis=-1, keepdims=True))
        student = exp_scores / jnp.sum(exp_scores, axis=0, keepdims=True)
        live = jnp.where(preact > 0, student * score_vec, 0.0)
        high = live.astype(BF16)
        part_ref[at, :] = high
        less_ref[at, :] = (live - high.astype(F32)).astype(BF16)
        return total + jnp.sum(student * hidden, axis=0, keepdims=True)

    gs_ref[...] = lax.fori_loop(0, requests, one, jnp.zeros((1, units), F32))
    step = min(256, feats)
    held = grad_refs[0].shape[0] // chunk

    def block(i, carry):
        at = pl.ds(pl.multiple_of(i * step, step), step)
        across = (((0,), (0,)), ((), ()))
        grad = lax.dot_general(x_ref[:, at], part_ref[...], across, preferred_element_type=F32)
        grad += lax.dot_general(x_ref[:, at], less_ref[...], across, preferred_element_type=F32)
        for j in range(step // chunk):
            piece = grad[j * chunk : (j + 1) * chunk, :]
            spot = order(i * (step // chunk) + j, me_ref[0])
            for half, ref in enumerate(grad_refs):

                @pl.when(spot // held == half)
                def _(ref=ref, half=half, piece=piece, spot=spot):
                    place = jnp.clip(spot - half * held, 0, held - 1)
                    ref[pl.ds(pl.multiple_of(place * chunk, chunk), chunk), :] = piece

        return carry

    lax.fori_loop(0, feats // step, block, 0)
    rated = c_ref[...].astype(F32) * e_ref[...].astype(F32)
    focus, wide = rate_ref.shape
    gangs = ATTENDER_GANGS
    head_row = lax.broadcasted_iota(jnp.int32, (focus, wide), 0) // (focus // gangs)
    head_col = lax.broadcasted_iota(jnp.int32, (focus, wide), 1) // (wide // gangs)
    same = (head_row == head_col).astype(F32).astype(BF16)
    high = rated.astype(BF16)
    middle = (rated - high.astype(F32)).astype(BF16)
    low = (rated - high.astype(F32) - middle.astype(F32)).astype(BF16)
    rate = jnp.dot(high, same, preferred_element_type=F32)
    rate += jnp.dot(middle, same, preferred_element_type=F32)
    rate += jnp.dot(low, same, preferred_element_type=F32)
    rate_ref[...] = rate.astype(BF16)


def student_part(x, w, s, content, rating, wide, me, pieces, halves, order):
    requests, cand, feats = x.shape
    units = w.shape[1]
    rows = requests * cand
    return pl.pallas_call(
        functools.partial(student_kernel, requests, feats // pieces, order),
        out_shape=(jax.ShapeDtypeStruct((feats // halves, units), F32),) * halves
        + (
            jax.ShapeDtypeStruct((1, units), F32),
            jax.ShapeDtypeStruct((content.shape[0], wide), BF16),
        ),
        in_specs=[scalars()] + [full_vmem()] * 5,
        out_specs=(full_vmem(),) * (halves + 2),
        scratch_shapes=[VMEM((rows, units), BF16)] * 2,
        compiler_params=room(20),
        cost_estimate=pl.CostEstimate(
            flops=4 * requests * cand * feats * units, bytes_accessed=8 * 10**6, transcendentals=0
        ),
    )(me, x.reshape(rows, feats), w, s.reshape(1, units), content, rating.reshape(1, -1))


def block_scores(dims, me, payload, ask, look, rate):
    requests, hist_slots, kept, tops, gangs = dims
    focus = look.shape[0]
    span = look.shape[1] // gangs
    hist_rows, kept_rows, pieces, meta_at = rows_of(
        requests, hist_slots, kept, ask.shape[0], focus
    )
    hist = payload[:hist_rows, :]
    keys = jnp.dot(hist, look[...], preferred_element_type=F32).astype(BF16)
    values = jnp.dot(hist, rate[...], preferred_element_type=F32)
    queries = None
    for p in range(pieces):
        rows = payload[hist_rows + p * kept_rows : hist_rows + (p + 1) * kept_rows, :]
        part = jnp.dot(rows, ask[p * focus : (p + 1) * focus, :], preferred_element_type=F32)
        queries = part if queries is None else queries + part
    queries = (queries * span**-0.5).astype(BF16)
    wide = gangs * kept
    head_row = lax.broadcasted_iota(jnp.int32, (wide, look.shape[1]), 0) // kept
    head_col = lax.broadcasted_iota(jnp.int32, (wide, look.shape[1]), 1) // span
    same_head = head_row == head_col
    slot = lax.broadcasted_iota(jnp.int32, (hist_slots, wide), 0).astype(F32)
    meta = payload[meta_at : meta_at + META_ROWS, :].astype(F32)
    meta_lane = lax.broadcasted_iota(jnp.int32, meta.shape, 1)
    hit = jnp.where((meta_lane < tops) & (meta == me.astype(F32)), 1.0, 0.0)
    routed = jnp.max(hit, axis=-1, keepdims=True)
    lengths = jnp.sum(jnp.where(meta_lane == tops, meta, 0.0), axis=-1, keepdims=True)
    lane = lax.broadcasted_iota(jnp.int32, (1, kept_rows), 1) // kept
    scores = jnp.zeros((1, kept_rows), F32)
    for r in range(requests):
        q = queries[r * kept : (r + 1) * kept, :]
        q_wide = jnp.where(same_head, jnp.concatenate([q] * gangs, axis=0), jnp.zeros((), BF16))
        logits = lax.dot_general(
            keys[r * hist_slots : (r + 1) * hist_slots, :],
            q_wide,
            (((1,), (1,)), ((), ())),
            preferred_element_type=F32,
        )
        weights = jnp.where(slot < lengths[r : r + 1, :], jnp.exp(logits), 0.0)
        mixed = weights * values[r * hist_slots : (r + 1) * hist_slots, :]
        per_head = jnp.sum(mixed, axis=0, keepdims=True) / jnp.sum(weights, axis=0, keepdims=True)
        folded = per_head[:, :kept_rows]
        for b in range(1, wide // kept_rows):
            folded = folded + per_head[:, b * kept_rows : (b + 1) * kept_rows]
        shift = kept
        while shift < kept_rows:
            folded = folded + pltpu.roll(folded, shift, 1)
            shift *= 2
        scores = jnp.where((lane == r) & (routed[r : r + 1, :] > 0), folded, scores)
    return scores


def own_columns(me, rows_of_piece, sel_rows):
    focus = rows_of_piece[0].shape[1]
    own = None
    for p, rows in enumerate(rows_of_piece):
        feature = lax.broadcasted_iota(jnp.int32, (sel_rows, focus), 1) + p * focus
        wanted = lax.broadcasted_iota(jnp.int32, (sel_rows, focus), 0) + me * sel_rows
        pick = (feature == wanted).astype(F32).astype(BF16)
        got = lax.dot_general(pick, rows, (((1,), (1,)), ((), ())), preferred_element_type=F32)
        own = got if own is None else own + got
    return own.astype(BF16)


def rank_kernel(dims, sel_rows, layout, wants, first, info_ref, *refs):
    want_scores, want_hidden, parts = wants
    requests, hist_slots, kept, _, _ = dims
    n_in = sum(sum(pieces) for pieces in layout) if layout else 1
    arrays, refs = refs[:n_in], refs[n_in:]
    if want_scores:
        (a_ref, l_ref, r_ref), refs = refs[:3], refs[3:]
    if want_hidden:
        w_ref, refs = refs[0], refs[1:]
    if parts is not None:
        earlier, gs_ref, refs = refs[: len(parts)], refs[len(parts)], refs[len(parts) + 1 :]
    if want_scores:
        o_ref, refs = refs[0], refs[1:]
    if want_hidden:
        h_ref, s_ref, refs = refs[0], refs[1], refs[2:]
    buf, sems = refs
    blocks, _, focus = buf.shape
    feats = (a_ref if want_scores else w_ref).shape[0]
    hist_rows, kept_rows, pieces, _ = rows_of(requests, hist_slots, kept, feats, focus)
    low = 0 if want_scores else hist_rows
    high = low + buf.shape[1]

    def start_block(b):
        if not layout:
            fetch(arrays[0].at[b, pl.ds(low, high - low), :], buf.at[b], sems.at[b])
            return
        at, i = 0, sum(sum(pieces) for pieces in layout[:b])
        for choices in layout[b]:
            rows = arrays[i].shape[0]
            begin, end = max(at, low), min(at + rows, high)
            if begin < end:
                for choice in range(choices):

                    def start(array=arrays[i + choice], at=at, begin=begin, end=end):
                        fetch(
                            array.at[pl.ds(begin - at, end - begin), :],
                            buf.at[b, pl.ds(begin - low, end - begin), :],
                            sems.at[b],
                        )

                    if choices == 1:
                        start()
                    else:
                        pl.when(info_ref[3] == choice)(start)
            at += rows
            i += choices

    def wait_block(b):
        pltpu.make_async_copy(buf.at[b], buf.at[b], sems.at[b]).wait()

    for b in range(blocks):
        start_block(b)
    if parts is not None:
        slot = 0
        for ref, count in zip(earlier, parts):
            for b in range(count):
                o_ref[pl.ds(info_ref[1] ^ slot, 1), :] = ref[b]
                slot += 1
        scored, lanes = slot + blocks, o_ref.shape[1]
        for i in range(o_ref.shape[0] - scored):
            o_ref[scored + i : scored + i + 1, :] = gs_ref[:, i * lanes : (i + 1) * lanes]
    me = info_ref[0]
    if want_scores:

        def one(b, carry):
            wait_block(b)
            row = block_scores(dims, me, buf.at[b], a_ref, l_ref, r_ref)
            if parts is not None:
                o_ref[pl.ds(info_ref[1] ^ (first + b), 1), :] = row
            else:
                o_ref[b] = row
            return carry

        lax.fori_loop(0, blocks, one, 0)
    else:
        for b in range(blocks):
            wait_block(b)
    if want_hidden:
        rows_of_piece = []
        for p in range(pieces):
            at = hist_rows - low + p * kept_rows
            rows_of_piece.append(
                jnp.concatenate([buf[b, at : at + kept_rows, :] for b in range(blocks)], axis=0)
            )
        preact = None
        for p, rows in enumerate(rows_of_piece):
            part = jnp.dot(
                rows, w_ref[p * focus : (p + 1) * focus, :], preferred_element_type=F32
            )
            preact = part if preact is None else preact + part
        h_ref[...] = jnp.maximum(preact, 0.0).astype(BF16)
        s_ref[...] = own_columns(me, rows_of_piece, sel_rows)


def rank(dims, me, payloads, score_weights, hidden_weights, sel_rows, first=0, message=None):
    requests, _, kept, _, _ = dims
    kept_rows = requests * kept
    want_scores, want_hidden = score_weights is not None, hidden_weights is not None
    if isinstance(payloads, list):
        blocks = len(payloads)
        payloads = [[p if isinstance(p, tuple) else (p,) for p in block] for block in payloads]
        layout = [[len(p) for p in block] for block in payloads]
        arrays = [a for block in payloads for p in block for a in p]
        rows, focus = sum(p[0].shape[0] for p in payloads[0]), arrays[0].shape[1]
    else:
        blocks, rows, focus = payloads.shape
        layout, arrays = None, [payloads]
    if not want_scores:
        rows = kept_rows * (hidden_weights[0].shape[0] // focus)
    scratch = [VMEM((blocks, rows, focus), BF16), pltpu.SemaphoreType.DMA((blocks,))]
    weights = list(score_weights or ()) + list(hidden_weights or ())
    shapes, outs, small, parts = [], [], [], None
    if want_scores:
        if message is None:
            shapes.append(jax.ShapeDtypeStruct((blocks, 1, kept_rows), F32))
        else:
            earlier, gs = message
            parts = [e.shape[0] for e in earlier]
            small = list(earlier) + [gs]
            total = sum(parts) + blocks + gs.shape[1] // kept_rows
            shapes.append(jax.ShapeDtypeStruct((total, kept_rows), F32))
        outs.append(full_vmem())
    if want_hidden:
        units = hidden_weights[0].shape[1]
        shapes.append(jax.ShapeDtypeStruct((blocks * kept_rows, units), BF16))
        shapes.append(jax.ShapeDtypeStruct((sel_rows, blocks * kept_rows), BF16))
        outs += [full_vmem()] * 2
    flops = blocks * (7 * 10**8 * want_scores + 3 * 10**8 * want_hidden)
    return pl.pallas_call(
        functools.partial(
            rank_kernel, dims, sel_rows, layout, (want_scores, want_hidden, parts), first
        ),
        out_shape=tuple(shapes),
        in_specs=[scalars()]
        + [in_place()] * len(arrays)
        + [full_vmem()] * (len(weights) + len(small)),
        out_specs=tuple(outs),
        scratch_shapes=scratch,
        compiler_params=room(22),
        cost_estimate=pl.CostEstimate(
            flops=flops, bytes_accessed=blocks * 10**6, transcendentals=0
        ),
    )(me, *arrays, *weights, *small)


def target_kernel(kept, tops, n_parts, me_ref, got_ref, s_ref, base_ref, *refs):
    sel_refs, hid_refs = refs[:n_parts], refs[n_parts : 2 * n_parts]
    out_ref, short_ref, target_ref = refs[2 * n_parts :]
    kept_rows = got_ref.shape[1]
    units = s_ref.shape[1]
    blocks = got_ref.shape[0] - units // kept_rows
    sel_rows = sel_refs[0].shape[0]
    total = got_ref[...]
    exp_teacher = jnp.exp(total[:blocks, :] / tops)
    near = lax.broadcasted_iota(jnp.int32, (kept_rows, kept_rows), 0) // kept
    far = lax.broadcasted_iota(jnp.int32, (kept_rows, kept_rows), 1) // kept
    group = (near == far).astype(F32)
    sums = jnp.dot(
        exp_teacher, group, preferred_element_type=F32, precision=lax.Precision.HIGHEST
    )
    target_ref[...] = exp_teacher / sums
    grad = jnp.zeros((sel_rows, units), F32)
    lift = jnp.zeros((1, units), F32)
    slot = 0
    for sel_ref, hid_ref in zip(sel_refs, hid_refs):
        count = sel_ref.shape[1] // kept_rows
        target = jnp.concatenate(
            [target_ref[pl.ds(me_ref[1] ^ (slot + b), 1), :] for b in range(count)], axis=1
        )
        high = target.astype(BF16).astype(F32)
        hidden = hid_ref[...]
        slot += count
        live = jnp.where(hidden > 0, jnp.ones((), BF16), jnp.zeros((), BF16))
        scaled = sel_ref[...].astype(F32) * target
        upper = scaled.astype(BF16)
        lower = (scaled - upper.astype(F32)).astype(BF16)
        halves = jnp.dot(
            jnp.concatenate([upper, lower], axis=0), live, preferred_element_type=F32
        )
        grad += halves[:sel_rows, :] + halves[sel_rows:, :]
        both = jnp.concatenate([high, target - high], axis=0).astype(BF16)
        pair = jnp.dot(both, hidden, preferred_element_type=F32)
        lift += pair[0:1, :] + pair[1:2, :]
    out_ref[:sel_rows, :] = -grad * s_ref[...].astype(F32)
    held = base_ref.shape[0]
    at = pl.ds(pl.multiple_of(me_ref[2] * held, 8), held)
    out_ref[at, :] = out_ref[at, :] + base_ref[...]
    for i in range(units // kept_rows):
        at = slice(i * kept_rows, (i + 1) * kept_rows)
        out_ref[sel_rows : sel_rows + 1, at] = total[blocks + i : blocks + i + 1, :] - lift[:, at]
    out_ref[sel_rows + 1 :, :] = jnp.zeros((out_ref.shape[0] - sel_rows - 1, units), F32)
    row = out_ref[sel_rows : sel_rows + 1, :]
    short_ref[...] = out_ref[...].astype(BF16)
    short_ref[sel_rows + 1 : sel_rows + 2, :] = (row - row.astype(BF16).astype(F32)).astype(BF16)


def target_part(kept, tops, me, got, hiddens, owns, s, base):
    sel_rows = owns[0].shape[0]
    units = hiddens[0].shape[1]
    blocks = got.shape[0] - units // got.shape[1]
    parts = len(hiddens)
    return pl.pallas_call(
        functools.partial(target_kernel, kept, tops, parts),
        out_shape=tuple(jax.ShapeDtypeStruct((sel_rows + 8, units), t) for t in (F32, BF16)),
        in_specs=[scalars()] + [full_vmem()] * (3 + 2 * parts),
        out_specs=(full_vmem(),) * 2,
        scratch_shapes=[VMEM((blocks, got.shape[1]), F32)],
        compiler_params=room(22),
        cost_estimate=pl.CostEstimate(flops=10**9, bytes_accessed=6 * 10**6, transcendentals=0),
    )(me, got, s.reshape(1, units), base, *owns, *hiddens)


def along(pairs):
    table = []
    for z, z_to in pairs:
        for low in range(4):
            table.append((4 * z + low, 4 * z_to + low))
    return table


def flip(bits):
    return [(i, i ^ bits) for i in range(16)]


SIBLING, Y_OVER, Z_NEAR, Z_FAR = flip(1), flip(2), flip(4), flip(8)
Z_INNER = along([(1, 2), (2, 1)])
Z_OUT = along([(1, 0), (2, 3)])


def shift(x, table, axis="shard"):
    return lax.ppermute(x, axis, table)


def gather_stages(b, inner, cut):
    near = shift(b, Z_NEAR)
    over = shift(b, Y_OVER)
    mid = shift(b, Z_INNER)
    mid_far = shift(near, Z_INNER)
    out_far = shift(mid, Z_OUT)
    over_near = shift(near, Y_OVER)
    far = jnp.where(inner, mid_far, out_far)
    out_last = shift(mid_far, Z_OUT)
    over_far = shift(far, Y_OVER)
    last = [jnp.where(inner, mid[:cut], out_last[:cut]), jnp.where(inner, mid[cut:], out_last[cut:])]
    over_last = shift(last[0], Y_OVER)
    rest_out = shift(over_far[cut:], Z_OUT)
    rest_mid = shift(over[cut:], Z_INNER)

    def beside(p):
        if isinstance(p, tuple):
            return tuple(shift(a, SIBLING) for a in p)
        return shift(p, SIBLING)

    def both(*pieces):
        return [list(pieces), [beside(p) for p in pieces]]

    return [
        both(b) + both(over) + both(near),
        both(over_near) + both(far),
        both(over_far) + both(*last),
        both(over_last, (rest_out, rest_mid)),
    ]


def halving_order(block, me):
    away = block ^ me
    z1, z0, y, core, grp = [(away >> i) & 1 for i in (4, 3, 2, 1, 0)]
    return (core << 4) | (grp << 3) | (z0 << 2) | (y << 1) | z1


def halve(keep, sent):
    for table, axis in (
        (SIBLING, "shard"),
        ([(0, 1), (1, 0)], "group"),
        (Z_NEAR, "shard"),
        (Y_OVER, "shard"),
        (Z_FAR, "shard"),
    ):
        wide = axis == "group" or table is SIBLING
        got = shift(sent if wide else sent.astype(BF16), table, axis).astype(F32)
        half = keep.shape[0] // 2
        if table is Z_FAR:
            return keep + got
        keep, sent = keep[:half] + got[:half], keep[half:] + got[half:]


def sum_over_shard(x):
    for table in (SIBLING, Y_OVER):
        got = shift(x, table)
        x = x + got
    near, far, last = shift(x, Z_NEAR), shift(x, Z_FAR), shift(x, flip(12))
    return (x + near) + (far + last)


def sum_kernel(a_ref, b_ref, grad_ref, score_ref):
    rows = grad_ref.shape[0]
    grad_ref[...] = a_ref[:rows, :] + b_ref[:rows, :].astype(F32)
    pair = b_ref[rows : rows + 2, :].astype(F32)
    score_ref[...] = a_ref[rows : rows + 1, :] + (pair[0:1, :] + pair[1:2, :])


def sum_two(a, b, rows):
    return pl.pallas_call(
        sum_kernel,
        out_shape=(
            jax.ShapeDtypeStruct((rows, a.shape[1]), F32),
            jax.ShapeDtypeStruct((1, a.shape[1]), F32),
        ),
        in_specs=[full_vmem()] * 2,
        out_specs=(full_vmem(),) * 2,
        compiler_params=room(4),
    )(a, b)


def body(
    offer_attribute_matrix,
    kept_offers,
    expert_target,
    sequence_extent,
    behaviour_sequence,
    inner_projection_matrix,
    student_rating_vector,
    asking_matrix,
    lookup_matrix,
    content_matrix,
    expert_rating_vector,
):
    requests, _, feats = offer_attribute_matrix.shape
    kept = kept_offers.shape[1]
    hist_slots, _ = behaviour_sequence.shape[1:]
    tops = expert_target.shape[1]
    units = inner_projection_matrix.shape[1]
    n_shard = lax.axis_size("shard")
    sel_rows = feats // n_shard
    me = lax.axis_index("shard")
    n_group = lax.axis_size("group")
    grp = lax.axis_index("group")

    payload = pack(
        offer_attribute_matrix, kept_offers, behaviour_sequence, expert_target, sequence_extent
    )
    linked = n_shard == 16 and n_group == 2
    place = (me * n_group + grp if linked else me).astype(jnp.int32).reshape(1)
    stack = (
        offer_attribute_matrix,
        inner_projection_matrix,
        student_rating_vector,
        content_matrix[0],
        expert_rating_vector[0],
        ATTENDER_GANGS * kept,
        place,
    )
    if linked:
        inner = ((me >> 2) ^ (me >> 3)) & 1
        stages = gather_stages(payload, inner == 1, requests * hist_slots)
        keep, sent, gs_student, rate = student_part(
            *stack, n_shard * n_group, 2, halving_order
        )
        base = halve(keep, sent)
        info = jnp.stack([me, me, grp, inner]).astype(jnp.int32)
    else:
        payloads = lax.all_gather(payload, "shard", axis=0, tiled=False)
        stages = [payloads[b : b + 4] for b in range(0, n_shard, 4)]
        grad_student, gs_student, rate = student_part(
            *stack, n_shard, 1, lambda block, at: block
        )
        base = lax.psum_scatter(grad_student, "shard", scatter_dimension=0, tiled=True)
        info = jnp.stack([me, 0 * me, 0 * me, 0 * me]).astype(jnp.int32)

    dims = (requests, hist_slots, kept, tops, ATTENDER_GANGS)
    score_weights = (asking_matrix[0], lookup_matrix[0], rate)
    hidden_weights = (inner_projection_matrix,)
    scores, hiddens, owns = [], [], []
    late = len(stages) - 2 if linked else len(stages) - 1
    for number, stage in enumerate(stages[:-1]):
        if number < late:
            score, hidden, own = rank(dims, info, stage, score_weights, hidden_weights, sel_rows)
            hiddens.append(hidden)
            owns.append(own)
        else:
            (score,) = rank(dims, info, stage, score_weights, None, sel_rows)
        scores.append(score)
    known = sum(s.shape[0] for s in scores)
    (send,) = rank(
        dims, info, stages[-1], score_weights, None, sel_rows, known, (scores, gs_student)
    )
    rest = stages[-2] + stages[-1] if linked else stages[-1]
    hidden, own = rank(dims, info, rest, None, hidden_weights, sel_rows)
    hiddens.append(hidden)
    owns.append(own)
    got = sum_over_shard(send) if linked else lax.psum(send, "shard")
    mine, short = target_part(kept, tops, info, got, hiddens, owns, student_rating_vector, base)
    if linked:
        grad, lift = sum_two(mine, shift(short, [(0, 1), (1, 0)], "group"), sel_rows)
        return grad, lift.reshape(units)
    whole = lax.psum(mine, "group")
    return whole[:sel_rows], whole[sel_rows]


def solution(mesh):
    placed = (
        P(("group", "shard"), None, None),
        P(("group", "shard"), None),
        P(("group", "shard"), None),
        P(("group", "shard")),
        P(("group", "shard"), None, None),
        P(),
        P(),
        P("shard", None, None),
        P("shard", None, None),
        P("shard", None, None),
        P("shard", None),
    )
    return jax.shard_map(
        body, mesh=mesh, in_specs=placed, out_specs=(P("shard", None), P()), check_vma=False
    )
```

```python
import functools

import jax
import jax.numpy as jnp
from jax import lax
from jax.experimental import pallas as pl
from jax.experimental.pallas import tpu as pltpu
from jax.sharding import PartitionSpec as P


ATTENDER_GANGS = 8
META_ROWS = 16
VMEM = pltpu.VMEM
F32 = jnp.float32
BF16 = jnp.bfloat16


def full_vmem():
    return pl.BlockSpec(memory_space=pltpu.VMEM)


def in_place():
    return pl.BlockSpec(memory_space=pl.ANY)


def scalars():
    return pl.BlockSpec(memory_space=pltpu.SMEM)


def room(mib):
    return pltpu.CompilerParams(vmem_limit_bytes=mib * 2**20)


def stays(x):
    return pltpu.with_memory_space_constraint(x, pltpu.HBM)


def fetch(source, target, sem):
    copy = pltpu.make_async_copy(source, target, sem)
    copy.start()
    return copy.wait


def rows_of(requests, hist_slots, kept, feature_span, focus_span):
    hist_rows = requests * hist_slots
    kept_rows = requests * kept
    pieces = feature_span // focus_span
    return hist_rows, kept_rows, pieces, hist_rows + kept_rows * pieces


def pack_kernel(
    target_ref, extent_ref, x_hbm, kept_ref, hist_hbm, out_hbm, x_ref, out_ref, sems
):
    requests, cand, _ = x_ref.shape
    kept = kept_ref.shape[1]
    focus = hist_hbm.shape[1]
    hist_rows = hist_hbm.shape[0]
    tops = target_ref.shape[1]
    pieces = x_ref.shape[2] // focus
    meta_at = hist_rows + pieces * requests * kept
    wait_hist = fetch(hist_hbm, out_ref.at[pl.ds(0, hist_rows), :], sems.at[requests])
    waits = [fetch(x_hbm.at[r], x_ref.at[r], sems.at[r]) for r in range(requests)]
    row = lax.broadcasted_iota(jnp.int32, (META_ROWS, focus), 0)
    lane = lax.broadcasted_iota(jnp.int32, (META_ROWS, focus), 1)
    meta = jnp.zeros((META_ROWS, focus), jnp.int32)
    for r in range(requests):
        for t in range(tops):
            meta = jnp.where((row == r) & (lane == t), target_ref[r, t], meta)
        meta = jnp.where((row == r) & (lane == tops), extent_ref[r], meta)
    out_ref[meta_at:, :] = meta.astype(F32).astype(BF16)
    wait_hist()
    at = pl.ds(0, hist_rows)
    wait_out = fetch(out_ref.at[at, :], out_hbm.at[at, :], sems.at[requests])
    for r in range(requests):
        waits[r]()
        cand_of = lax.broadcasted_iota(jnp.int32, (cand, kept), 0)
        pick = (cand_of == kept_ref[r : r + 1, :]).astype(F32).astype(BF16)
        for p in range(pieces):
            rows = lax.dot_general(
                pick,
                x_ref[r, :, p * focus : (p + 1) * focus],
                (((0,), (0,)), ((), ())),
                preferred_element_type=F32,
            )
            at = hist_rows + p * requests * kept + r * kept
            out_ref[at : at + kept, :] = rows.astype(BF16)
    at = pl.ds(hist_rows, out_ref.shape[0] - hist_rows)
    wait_rest = fetch(out_ref.at[at, :], out_hbm.at[at, :], sems.at[0])
    wait_out()
    wait_rest()


def pack(x, kept, hist, targets, extents):
    requests, _, feats = x.shape
    focus = hist.shape[2]
    flat_hist = hist.reshape(-1, focus)
    total = rows_of(requests, hist.shape[1], kept.shape[1], feats, focus)[3] + META_ROWS
    return pl.pallas_call(
        pack_kernel,
        out_shape=jax.ShapeDtypeStruct((total, focus), BF16),
        in_specs=[scalars(), scalars(), in_place(), full_vmem(), in_place()],
        out_specs=in_place(),
        scratch_shapes=[
            VMEM(x.shape, BF16),
            VMEM((total, focus), BF16),
            pltpu.SemaphoreType.DMA((requests + 1,)),
        ],
        cost_estimate=pl.CostEstimate(flops=10**8, bytes_accessed=3 * 10**6, transcendentals=0),
    )(targets, extents, stays(x), stays(kept), stays(flat_hist))


def student_kernel(requests, chunk, order, me_ref, x_ref, w_ref, s_ref, c_ref, e_ref, *refs):
    grad_refs, (gs_ref, rate_ref, part_ref, less_ref) = refs[:-4], refs[-4:]
    rows, feats = x_ref.shape
    units = w_ref.shape[1]
    cand = rows // requests
    score_vec = s_ref[...].astype(F32)

    def one(r, total):
        at = pl.ds(pl.multiple_of(r * cand, cand), cand)
        preact = jnp.dot(x_ref[at, :], w_ref[...], preferred_element_type=F32)
        hidden = jnp.maximum(preact, 0.0)
        exp_scores = jnp.exp(jnp.sum(hidden * score_vec, axis=-1, keepdims=True))
        student = exp_scores / jnp.sum(exp_scores, axis=0, keepdims=True)
        live = jnp.where(preact > 0, student * score_vec, 0.0)
        high = live.astype(BF16)
        part_ref[at, :] = high
        less_ref[at, :] = (live - high.astype(F32)).astype(BF16)
        return total + jnp.sum(student * hidden, axis=0, keepdims=True)

    gs_ref[...] = lax.fori_loop(0, requests, one, jnp.zeros((1, units), F32))
    step = min(256, feats)
    held = grad_refs[0].shape[0] // chunk

    def block(i, carry):
        at = pl.ds(pl.multiple_of(i * step, step), step)
        across = (((0,), (0,)), ((), ()))
        grad = lax.dot_general(x_ref[:, at], part_ref[...], across, preferred_element_type=F32)
        grad += lax.dot_general(x_ref[:, at], less_ref[...], across, preferred_element_type=F32)
        for j in range(step // chunk):
            piece = grad[j * chunk : (j + 1) * chunk, :]
            spot = order(i * (step // chunk) + j, me_ref[0])
            for half, ref in enumerate(grad_refs):

                @pl.when(spot // held == half)
                def _(ref=ref, half=half, piece=piece, spot=spot):
                    place = jnp.clip(spot - half * held, 0, held - 1)
                    ref[pl.ds(pl.multiple_of(place * chunk, chunk), chunk), :] = piece

        return carry

    lax.fori_loop(0, feats // step, block, 0)
    rated = c_ref[...].astype(F32) * e_ref[...].astype(F32)
    focus, wide = rate_ref.shape
    gangs = ATTENDER_GANGS
    head_row = lax.broadcasted_iota(jnp.int32, (focus, wide), 0) // (focus // gangs)
    head_col = lax.broadcasted_iota(jnp.int32, (focus, wide), 1) // (wide // gangs)
    same = (head_row == head_col).astype(F32).astype(BF16)
    high = rated.astype(BF16)
    middle = (rated - high.astype(F32)).astype(BF16)
    low = (rated - high.astype(F32) - middle.astype(F32)).astype(BF16)
    rate = jnp.dot(high, same, preferred_element_type=F32)
    rate += jnp.dot(middle, same, preferred_element_type=F32)
    rate += jnp.dot(low, same, preferred_element_type=F32)
    rate_ref[...] = rate.astype(BF16)


def student_part(x, w, s, content, rating, wide, me, pieces, halves, order):
    requests, cand, feats = x.shape
    units = w.shape[1]
    rows = requests * cand
    return pl.pallas_call(
        functools.partial(student_kernel, requests, feats // pieces, order),
        out_shape=(jax.ShapeDtypeStruct((feats // halves, units), F32),) * halves
        + (
            jax.ShapeDtypeStruct((1, units), F32),
            jax.ShapeDtypeStruct((content.shape[0], wide), BF16),
        ),
        in_specs=[scalars()] + [full_vmem()] * 5,
        out_specs=(full_vmem(),) * (halves + 2),
        scratch_shapes=[VMEM((rows, units), BF16)] * 2,
        compiler_params=room(20),
        cost_estimate=pl.CostEstimate(
            flops=4 * requests * cand * feats * units, bytes_accessed=8 * 10**6, transcendentals=0
        ),
    )(me, x.reshape(rows, feats), w, s.reshape(1, units), content, rating.reshape(1, -1))


def block_scores(dims, me, payload, ask, look, rate):
    requests, hist_slots, kept, tops, gangs = dims
    focus = look.shape[0]
    span = look.shape[1] // gangs
    hist_rows, kept_rows, pieces, meta_at = rows_of(
        requests, hist_slots, kept, ask.shape[0], focus
    )
    hist = payload[:hist_rows, :]
    keys = jnp.dot(hist, look[...], preferred_element_type=F32).astype(BF16)
    values = jnp.dot(hist, rate[...], preferred_element_type=F32)
    queries = None
    for p in range(pieces):
        rows = payload[hist_rows + p * kept_rows : hist_rows + (p + 1) * kept_rows, :]
        part = jnp.dot(rows, ask[p * focus : (p + 1) * focus, :], preferred_element_type=F32)
        queries = part if queries is None else queries + part
    queries = (queries * span**-0.5).astype(BF16)
    wide = gangs * kept
    head_row = lax.broadcasted_iota(jnp.int32, (wide, look.shape[1]), 0) // kept
    head_col = lax.broadcasted_iota(jnp.int32, (wide, look.shape[1]), 1) // span
    same_head = head_row == head_col
    slot = lax.broadcasted_iota(jnp.int32, (hist_slots, wide), 0).astype(F32)
    meta = payload[meta_at : meta_at + META_ROWS, :].astype(F32)
    meta_lane = lax.broadcasted_iota(jnp.int32, meta.shape, 1)
    hit = jnp.where((meta_lane < tops) & (meta == me.astype(F32)), 1.0, 0.0)
    routed = jnp.max(hit, axis=-1, keepdims=True)
    lengths = jnp.sum(jnp.where(meta_lane == tops, meta, 0.0), axis=-1, keepdims=True)
    lane = lax.broadcasted_iota(jnp.int32, (1, kept_rows), 1) // kept
    scores = jnp.zeros((1, kept_rows), F32)
    for r in range(requests):
        q = queries[r * kept : (r + 1) * kept, :]
        q_wide = jnp.where(same_head, jnp.concatenate([q] * gangs, axis=0), jnp.zeros((), BF16))
        logits = lax.dot_general(
            keys[r * hist_slots : (r + 1) * hist_slots, :],
            q_wide,
            (((1,), (1,)), ((), ())),
            preferred_element_type=F32,
        )
        weights = jnp.where(slot < lengths[r : r + 1, :], jnp.exp(logits), 0.0)
        mixed = weights * values[r * hist_slots : (r + 1) * hist_slots, :]
        per_head = jnp.sum(mixed, axis=0, keepdims=True) / jnp.sum(weights, axis=0, keepdims=True)
        folded = per_head[:, :kept_rows]
        for b in range(1, wide // kept_rows):
            folded = folded + per_head[:, b * kept_rows : (b + 1) * kept_rows]
        shift = kept
        while shift < kept_rows:
            folded = folded + pltpu.roll(folded, shift, 1)
            shift *= 2
        scores = jnp.where((lane == r) & (routed[r : r + 1, :] > 0), folded, scores)
    return scores


def own_columns(me, rows_of_piece, sel_rows):
    focus = rows_of_piece[0].shape[1]
    own = None
    for p, rows in enumerate(rows_of_piece):
        feature = lax.broadcasted_iota(jnp.int32, (sel_rows, focus), 1) + p * focus
        wanted = lax.broadcasted_iota(jnp.int32, (sel_rows, focus), 0) + me * sel_rows
        pick = (feature == wanted).astype(F32).astype(BF16)
        got = lax.dot_general(pick, rows, (((1,), (1,)), ((), ())), preferred_element_type=F32)
        own = got if own is None else own + got
    return own.astype(BF16)


def rank_kernel(dims, sel_rows, layout, wants, first, info_ref, *refs):
    want_scores, want_hidden, parts = wants
    requests, hist_slots, kept, _, _ = dims
    n_in = sum(sum(pieces) for pieces in layout) if layout else 1
    arrays, refs = refs[:n_in], refs[n_in:]
    if want_scores:
        (a_ref, l_ref, r_ref), refs = refs[:3], refs[3:]
    if want_hidden:
        w_ref, refs = refs[0], refs[1:]
    if parts is not None:
        earlier, gs_ref, refs = refs[: len(parts)], refs[len(parts)], refs[len(parts) + 1 :]
    if want_scores:
        o_ref, refs = refs[0], refs[1:]
    if want_hidden:
        h_ref, s_ref, refs = refs[0], refs[1], refs[2:]
    buf, sems = refs
    blocks, _, focus = buf.shape
    feats = (a_ref if want_scores else w_ref).shape[0]
    hist_rows, kept_rows, pieces, _ = rows_of(requests, hist_slots, kept, feats, focus)
    low = 0 if want_scores else hist_rows
    high = low + buf.shape[1]

    def start_block(b):
        if not layout:
            fetch(arrays[0].at[b, pl.ds(low, high - low), :], buf.at[b], sems.at[b])
            return
        at, i = 0, sum(sum(pieces) for pieces in layout[:b])
        for choices in layout[b]:
            rows = arrays[i].shape[0]
            begin, end = max(at, low), min(at + rows, high)
            if begin < end:
                for choice in range(choices):

                    def start(array=arrays[i + choice], at=at, begin=begin, end=end):
                        fetch(
                            array.at[pl.ds(begin - at, end - begin), :],
                            buf.at[b, pl.ds(begin - low, end - begin), :],
                            sems.at[b],
                        )

                    if choices == 1:
                        start()
                    else:
                        pl.when(info_ref[3] == choice)(start)
            at += rows
            i += choices

    def wait_block(b):
        pltpu.make_async_copy(buf.at[b], buf.at[b], sems.at[b]).wait()

    for b in range(blocks):
        start_block(b)
    if parts is not None:
        slot = 0
        for ref, count in zip(earlier, parts):
            for b in range(count):
                o_ref[pl.ds(info_ref[1] ^ slot, 1), :] = ref[b]
                slot += 1
        scored, lanes = slot + blocks, o_ref.shape[1]
        for i in range(o_ref.shape[0] - scored):
            o_ref[scored + i : scored + i + 1, :] = gs_ref[:, i * lanes : (i + 1) * lanes]
    me = info_ref[0]
    if want_scores:

        def one(b, carry):
            wait_block(b)
            row = block_scores(dims, me, buf.at[b], a_ref, l_ref, r_ref)
            if parts is not None:
                o_ref[pl.ds(info_ref[1] ^ (first + b), 1), :] = row
            else:
                o_ref[b] = row
            return carry

        lax.fori_loop(0, blocks, one, 0)
    else:
        for b in range(blocks):
            wait_block(b)
    if want_hidden:
        rows_of_piece = []
        for p in range(pieces):
            at = hist_rows - low + p * kept_rows
            rows_of_piece.append(
                jnp.concatenate([buf[b, at : at + kept_rows, :] for b in range(blocks)], axis=0)
            )
        preact = None
        for p, rows in enumerate(rows_of_piece):
            part = jnp.dot(
                rows, w_ref[p * focus : (p + 1) * focus, :], preferred_element_type=F32
            )
            preact = part if preact is None else preact + part
        h_ref[...] = jnp.maximum(preact, 0.0).astype(BF16)
        s_ref[...] = own_columns(me, rows_of_piece, sel_rows)


def rank(dims, me, payloads, score_weights, hidden_weights, sel_rows, first=0, message=None):
    requests, _, kept, _, _ = dims
    kept_rows = requests * kept
    want_scores, want_hidden = score_weights is not None, hidden_weights is not None
    if isinstance(payloads, list):
        blocks = len(payloads)
        payloads = [[p if isinstance(p, tuple) else (p,) for p in block] for block in payloads]
        layout = [[len(p) for p in block] for block in payloads]
        arrays = [a for block in payloads for p in block for a in p]
        rows, focus = sum(p[0].shape[0] for p in payloads[0]), arrays[0].shape[1]
    else:
        blocks, rows, focus = payloads.shape
        layout, arrays = None, [payloads]
    if not want_scores:
        rows = kept_rows * (hidden_weights[0].shape[0] // focus)
    scratch = [VMEM((blocks, rows, focus), BF16), pltpu.SemaphoreType.DMA((blocks,))]
    weights = list(score_weights or ()) + list(hidden_weights or ())
    shapes, outs, small, parts = [], [], [], None
    if want_scores:
        if message is None:
            shapes.append(jax.ShapeDtypeStruct((blocks, 1, kept_rows), F32))
        else:
            earlier, gs = message
            parts = [e.shape[0] for e in earlier]
            small = list(earlier) + [gs]
            total = sum(parts) + blocks + gs.shape[1] // kept_rows
            shapes.append(jax.ShapeDtypeStruct((total, kept_rows), F32))
        outs.append(full_vmem())
    if want_hidden:
        units = hidden_weights[0].shape[1]
        shapes.append(jax.ShapeDtypeStruct((blocks * kept_rows, units), BF16))
        shapes.append(jax.ShapeDtypeStruct((sel_rows, blocks * kept_rows), BF16))
        outs += [full_vmem()] * 2
    flops = blocks * (7 * 10**8 * want_scores + 3 * 10**8 * want_hidden)
    return pl.pallas_call(
        functools.partial(
            rank_kernel, dims, sel_rows, layout, (want_scores, want_hidden, parts), first
        ),
        out_shape=tuple(shapes),
        in_specs=[scalars()]
        + [in_place()] * len(arrays)
        + [full_vmem()] * (len(weights) + len(small)),
        out_specs=tuple(outs),
        scratch_shapes=scratch,
        compiler_params=room(22),
        cost_estimate=pl.CostEstimate(
            flops=flops, bytes_accessed=blocks * 10**6, transcendentals=0
        ),
    )(me, *arrays, *weights, *small)


def target_kernel(kept, tops, n_parts, me_ref, got_ref, s_ref, base_ref, *refs):
    sel_refs, hid_refs = refs[:n_parts], refs[n_parts : 2 * n_parts]
    out_ref, short_ref, target_ref = refs[2 * n_parts :]
    kept_rows = got_ref.shape[1]
    units = s_ref.shape[1]
    blocks = got_ref.shape[0] - units // kept_rows
    sel_rows = sel_refs[0].shape[0]
    total = got_ref[...]
    exp_teacher = jnp.exp(total[:blocks, :] / tops)
    near = lax.broadcasted_iota(jnp.int32, (kept_rows, kept_rows), 0) // kept
    far = lax.broadcasted_iota(jnp.int32, (kept_rows, kept_rows), 1) // kept
    group = (near == far).astype(F32)
    sums = jnp.dot(
        exp_teacher, group, preferred_element_type=F32, precision=lax.Precision.HIGHEST
    )
    target_ref[...] = exp_teacher / sums
    grad = jnp.zeros((sel_rows, units), F32)
    lift = jnp.zeros((1, units), F32)
    slot = 0
    for sel_ref, hid_ref in zip(sel_refs, hid_refs):
        count = sel_ref.shape[1] // kept_rows
        target = jnp.concatenate(
            [target_ref[pl.ds(me_ref[1] ^ (slot + b), 1), :] for b in range(count)], axis=1
        )
        high = target.astype(BF16).astype(F32)
        hidden = hid_ref[...]
        slot += count
        live = jnp.where(hidden > 0, jnp.ones((), BF16), jnp.zeros((), BF16))
        scaled = sel_ref[...].astype(F32) * target
        upper = scaled.astype(BF16)
        lower = (scaled - upper.astype(F32)).astype(BF16)
        halves = jnp.dot(
            jnp.concatenate([upper, lower], axis=0), live, preferred_element_type=F32
        )
        grad += halves[:sel_rows, :] + halves[sel_rows:, :]
        both = jnp.concatenate([high, target - high], axis=0).astype(BF16)
        pair = jnp.dot(both, hidden, preferred_element_type=F32)
        lift += pair[0:1, :] + pair[1:2, :]
    out_ref[:sel_rows, :] = -grad * s_ref[...].astype(F32)
    held = base_ref.shape[0]
    at = pl.ds(pl.multiple_of(me_ref[2] * held, 8), held)
    out_ref[at, :] = out_ref[at, :] + base_ref[...]
    for i in range(units // kept_rows):
        at = slice(i * kept_rows, (i + 1) * kept_rows)
        out_ref[sel_rows : sel_rows + 1, at] = total[blocks + i : blocks + i + 1, :] - lift[:, at]
    out_ref[sel_rows + 1 :, :] = jnp.zeros((out_ref.shape[0] - sel_rows - 1, units), F32)
    row = out_ref[sel_rows : sel_rows + 1, :]
    short_ref[...] = out_ref[...].astype(BF16)
    short_ref[sel_rows + 1 : sel_rows + 2, :] = (row - row.astype(BF16).astype(F32)).astype(BF16)


def target_part(kept, tops, me, got, hiddens, owns, s, base):
    sel_rows = owns[0].shape[0]
    units = hiddens[0].shape[1]
    blocks = got.shape[0] - units // got.shape[1]
    parts = len(hiddens)
    return pl.pallas_call(
        functools.partial(target_kernel, kept, tops, parts),
        out_shape=tuple(jax.ShapeDtypeStruct((sel_rows + 8, units), t) for t in (F32, BF16)),
        in_specs=[scalars()] + [full_vmem()] * (3 + 2 * parts),
        out_specs=(full_vmem(),) * 2,
        scratch_shapes=[VMEM((blocks, got.shape[1]), F32)],
        compiler_params=room(22),
        cost_estimate=pl.CostEstimate(flops=10**9, bytes_accessed=6 * 10**6, transcendentals=0),
    )(me, got, s.reshape(1, units), base, *owns, *hiddens)


def along(pairs):
    table = []
    for z, z_to in pairs:
        for low in range(4):
            table.append((4 * z + low, 4 * z_to + low))
    return table


def flip(bits):
    return [(i, i ^ bits) for i in range(16)]


SIBLING, Y_OVER, Z_NEAR, Z_FAR = flip(1), flip(2), flip(4), flip(8)
Z_INNER = along([(1, 2), (2, 1)])
Z_OUT = along([(1, 0), (2, 3)])


def shift(x, table, axis="shard"):
    return lax.ppermute(x, axis, table)


def gather_stages(b, inner, cut):
    near = shift(b, Z_NEAR)
    over = shift(b, Y_OVER)
    mid = shift(b, Z_INNER)
    mid_far = shift(near, Z_INNER)
    out_far = shift(mid, Z_OUT)
    over_near = shift(near, Y_OVER)
    far = jnp.where(inner, mid_far, out_far)
    out_last = shift(mid_far, Z_OUT)
    over_far = shift(far, Y_OVER)
    last = [jnp.where(inner, mid[:cut], out_last[:cut]), jnp.where(inner, mid[cut:], out_last[cut:])]
    over_last = shift(last[0], Y_OVER)
    rest_out = shift(over_far[cut:], Z_OUT)
    rest_mid = shift(over[cut:], Z_INNER)

    def beside(p):
        if isinstance(p, tuple):
            return tuple(shift(a, SIBLING) for a in p)
        return shift(p, SIBLING)

    def both(*pieces):
        return [list(pieces), [beside(p) for p in pieces]]

    return [
        both(b) + both(over) + both(near),
        both(over_near) + both(far),
        both(over_far) + both(*last),
        both(over_last, (rest_out, rest_mid)),
    ]


def halving_order(block, me):
    away = block ^ me
    z1, z0, y, core, grp = [(away >> i) & 1 for i in (4, 3, 2, 1, 0)]
    return (core << 4) | (grp << 3) | (z0 << 2) | (y << 1) | z1


def halve(keep, sent):
    for table, axis in (
        (SIBLING, "shard"),
        ([(0, 1), (1, 0)], "group"),
        (Z_NEAR, "shard"),
        (Y_OVER, "shard"),
        (Z_FAR, "shard"),
    ):
        wide = axis == "group" or table is SIBLING
        got = shift(sent if wide else sent.astype(BF16), table, axis).astype(F32)
        half = keep.shape[0] // 2
        if table is Z_FAR:
            return keep + got
        keep, sent = keep[:half] + got[:half], keep[half:] + got[half:]


def sum_over_shard(x):
    for table in (SIBLING, Y_OVER):
        got = shift(x, table)
        x = x + got
    near, far, last = shift(x, Z_NEAR), shift(x, Z_FAR), shift(x, flip(12))
    return (x + near) + (far + last)


def sum_kernel(a_ref, b_ref, grad_ref, score_ref):
    rows = grad_ref.shape[0]
    grad_ref[...] = a_ref[:rows, :] + b_ref[:rows, :].astype(F32)
    pair = b_ref[rows : rows + 2, :].astype(F32)
    score_ref[...] = a_ref[rows : rows + 1, :] + (pair[0:1, :] + pair[1:2, :])


def sum_two(a, b, rows):
    return pl.pallas_call(
        sum_kernel,
        out_shape=(
            jax.ShapeDtypeStruct((rows, a.shape[1]), F32),
            jax.ShapeDtypeStruct((1, a.shape[1]), F32),
        ),
        in_specs=[full_vmem()] * 2,
        out_specs=(full_vmem(),) * 2,
        compiler_params=room(4),
    )(a, b)


def body(
    offer_attribute_matrix,
    kept_offers,
    expert_target,
    sequence_extent,
    behaviour_sequence,
    inner_projection_matrix,
    student_rating_vector,
    asking_matrix,
    lookup_matrix,
    content_matrix,
    expert_rating_vector,
):
    requests, _, feats = offer_attribute_matrix.shape
    kept = kept_offers.shape[1]
    hist_slots, _ = behaviour_sequence.shape[1:]
    tops = expert_target.shape[1]
    units = inner_projection_matrix.shape[1]
    n_shard = lax.axis_size("shard")
    sel_rows = feats // n_shard
    me = lax.axis_index("shard")
    n_group = lax.axis_size("group")
    grp = lax.axis_index("group")

    payload = pack(
        offer_attribute_matrix, kept_offers, behaviour_sequence, expert_target, sequence_extent
    )
    linked = n_shard == 16 and n_group == 2
    place = (me * n_group + grp if linked else me).astype(jnp.int32).reshape(1)
    stack = (
        offer_attribute_matrix,
        inner_projection_matrix,
        student_rating_vector,
        content_matrix[0],
        expert_rating_vector[0],
        ATTENDER_GANGS * kept,
        place,
    )
    if linked:
        inner = ((me >> 2) ^ (me >> 3)) & 1
        stages = gather_stages(payload, inner == 1, requests * hist_slots + META_ROWS)
        keep, sent, gs_student, rate = student_part(
            *stack, n_shard * n_group, 2, halving_order
        )
        base = halve(keep, sent)
        info = jnp.stack([me, me, grp, inner]).astype(jnp.int32)
    else:
        payloads = lax.all_gather(payload, "shard", axis=0, tiled=False)
        stages = [payloads[b : b + 4] for b in range(0, n_shard, 4)]
        grad_student, gs_student, rate = student_part(
            *stack, n_shard, 1, lambda block, at: block
        )
        base = lax.psum_scatter(grad_student, "shard", scatter_dimension=0, tiled=True)
        info = jnp.stack([me, 0 * me, 0 * me, 0 * me]).astype(jnp.int32)

    dims = (requests, hist_slots, kept, tops, ATTENDER_GANGS)
    score_weights = (asking_matrix[0], lookup_matrix[0], rate)
    hidden_weights = (inner_projection_matrix,)
    scores, hiddens, owns = [], [], []
    for stage in stages[:-1]:
        score, hidden, own = rank(dims, info, stage, score_weights, hidden_weights, sel_rows)
        hiddens.append(hidden)
        owns.append(own)
        scores.append(score)
    known = sum(s.shape[0] for s in scores)
    (send,) = rank(
        dims, info, stages[-1], score_weights, None, sel_rows, known, (scores, gs_student)
    )
    hidden, own = rank(dims, info, stages[-1], None, hidden_weights, sel_rows)
    hiddens.append(hidden)
    owns.append(own)
    got = sum_over_shard(send) if linked else lax.psum(send, "shard")
    mine, short = target_part(kept, tops, info, got, hiddens, owns, student_rating_vector, base)
    if linked:
        grad, lift = sum_two(mine, shift(short, [(0, 1), (1, 0)], "group"), sel_rows)
        return grad, lift.reshape(units)
    whole = lax.psum(mine, "group")
    return whole[:sel_rows], whole[sel_rows]


def solution(mesh):
    placed = (
        P(("group", "shard"), None, None),
        P(("group", "shard"), None),
        P(("group", "shard"), None),
        P(("group", "shard")),
        P(("group", "shard"), None, None),
        P(),
        P(),
        P("shard", None, None),
        P("shard", None, None),
        P("shard", None, None),
        P("shard", None),
    )
    return jax.shard_map(
        body, mesh=mesh, in_specs=placed, out_specs=(P("shard", None), P()), check_vma=False
    )
```

```python
import functools

import jax
import jax.numpy as jnp
from jax import lax
from jax.experimental import pallas as pl
from jax.experimental.pallas import tpu as pltpu
from jax.sharding import PartitionSpec as P


ATTENDER_GANGS = 8
META_ROWS = 16
VMEM = pltpu.VMEM
F32 = jnp.float32
BF16 = jnp.bfloat16


def full_vmem():
    return pl.BlockSpec(memory_space=pltpu.VMEM)


def in_place():
    return pl.BlockSpec(memory_space=pl.ANY)


def scalars():
    return pl.BlockSpec(memory_space=pltpu.SMEM)


def room(mib):
    return pltpu.CompilerParams(vmem_limit_bytes=mib * 2**20)


def stays(x):
    return pltpu.with_memory_space_constraint(x, pltpu.HBM)


def fetch(source, target, sem):
    copy = pltpu.make_async_copy(source, target, sem)
    copy.start()
    return copy.wait


def rows_of(requests, hist_slots, kept, feature_span, focus_span):
    hist_rows = requests * hist_slots
    kept_rows = requests * kept
    pieces = feature_span // focus_span
    return hist_rows, kept_rows, pieces, hist_rows + kept_rows * pieces


def pack_kernel(
    target_ref, extent_ref, x_hbm, kept_ref, hist_hbm, out_hbm, x_ref, out_ref, sems
):
    requests, cand, _ = x_ref.shape
    kept = kept_ref.shape[1]
    focus = hist_hbm.shape[1]
    hist_rows = hist_hbm.shape[0]
    tops = target_ref.shape[1]
    pieces = x_ref.shape[2] // focus
    meta_at = hist_rows + pieces * requests * kept
    wait_hist = fetch(hist_hbm, out_ref.at[pl.ds(0, hist_rows), :], sems.at[requests])
    waits = [fetch(x_hbm.at[r], x_ref.at[r], sems.at[r]) for r in range(requests)]
    row = lax.broadcasted_iota(jnp.int32, (META_ROWS, focus), 0)
    lane = lax.broadcasted_iota(jnp.int32, (META_ROWS, focus), 1)
    meta = jnp.zeros((META_ROWS, focus), jnp.int32)
    for r in range(requests):
        for t in range(tops):
            meta = jnp.where((row == r) & (lane == t), target_ref[r, t], meta)
        meta = jnp.where((row == r) & (lane == tops), extent_ref[r], meta)
    out_ref[meta_at:, :] = meta.astype(F32).astype(BF16)
    wait_hist()
    at = pl.ds(0, hist_rows)
    wait_out = fetch(out_ref.at[at, :], out_hbm.at[at, :], sems.at[requests])
    for r in range(requests):
        waits[r]()
        cand_of = lax.broadcasted_iota(jnp.int32, (cand, kept), 0)
        pick = (cand_of == kept_ref[r : r + 1, :]).astype(F32).astype(BF16)
        for p in range(pieces):
            rows = lax.dot_general(
                pick,
                x_ref[r, :, p * focus : (p + 1) * focus],
                (((0,), (0,)), ((), ())),
                preferred_element_type=F32,
            )
            at = hist_rows + p * requests * kept + r * kept
            out_ref[at : at + kept, :] = rows.astype(BF16)
    at = pl.ds(hist_rows, out_ref.shape[0] - hist_rows)
    wait_rest = fetch(out_ref.at[at, :], out_hbm.at[at, :], sems.at[0])
    wait_out()
    wait_rest()


def pack(x, kept, hist, targets, extents):
    requests, _, feats = x.shape
    focus = hist.shape[2]
    flat_hist = hist.reshape(-1, focus)
    total = rows_of(requests, hist.shape[1], kept.shape[1], feats, focus)[3] + META_ROWS
    return pl.pallas_call(
        pack_kernel,
        out_shape=jax.ShapeDtypeStruct((total, focus), BF16),
        in_specs=[scalars(), scalars(), in_place(), full_vmem(), in_place()],
        out_specs=in_place(),
        scratch_shapes=[
            VMEM(x.shape, BF16),
            VMEM((total, focus), BF16),
            pltpu.SemaphoreType.DMA((requests + 1,)),
        ],
        cost_estimate=pl.CostEstimate(flops=10**8, bytes_accessed=3 * 10**6, transcendentals=0),
    )(targets, extents, stays(x), stays(kept), stays(flat_hist))


def student_kernel(requests, chunk, order, me_ref, x_ref, w_ref, s_ref, c_ref, e_ref, *refs):
    grad_refs, (gs_ref, rate_ref, part_ref, less_ref) = refs[:-4], refs[-4:]
    rows, feats = x_ref.shape
    units = w_ref.shape[1]
    cand = rows // requests
    score_vec = s_ref[...].astype(F32)

    def one(r, total):
        at = pl.ds(pl.multiple_of(r * cand, cand), cand)
        preact = jnp.dot(x_ref[at, :], w_ref[...], preferred_element_type=F32)
        hidden = jnp.maximum(preact, 0.0)
        exp_scores = jnp.exp(jnp.sum(hidden * score_vec, axis=-1, keepdims=True))
        student = exp_scores / jnp.sum(exp_scores, axis=0, keepdims=True)
        live = jnp.where(preact > 0, student * score_vec, 0.0)
        high = live.astype(BF16)
        part_ref[at, :] = high
        less_ref[at, :] = (live - high.astype(F32)).astype(BF16)
        return total + jnp.sum(student * hidden, axis=0, keepdims=True)

    gs_ref[...] = lax.fori_loop(0, requests, one, jnp.zeros((1, units), F32))
    step = min(256, feats)
    held = grad_refs[0].shape[0] // chunk

    def block(i, carry):
        at = pl.ds(pl.multiple_of(i * step, step), step)
        across = (((0,), (0,)), ((), ()))
        grad = lax.dot_general(x_ref[:, at], part_ref[...], across, preferred_element_type=F32)
        grad += lax.dot_general(x_ref[:, at], less_ref[...], across, preferred_element_type=F32)
        for j in range(step // chunk):
            piece = grad[j * chunk : (j + 1) * chunk, :]
            spot = order(i * (step // chunk) + j, me_ref[0])
            for half, ref in enumerate(grad_refs):

                @pl.when(spot // held == half)
                def _(ref=ref, half=half, piece=piece, spot=spot):
                    place = jnp.clip(spot - half * held, 0, held - 1)
                    ref[pl.ds(pl.multiple_of(place * chunk, chunk), chunk), :] = piece

        return carry

    lax.fori_loop(0, feats // step, block, 0)
    rated = c_ref[...].astype(F32) * e_ref[...].astype(F32)
    focus, wide = rate_ref.shape
    gangs = ATTENDER_GANGS
    head_row = lax.broadcasted_iota(jnp.int32, (focus, wide), 0) // (focus // gangs)
    head_col = lax.broadcasted_iota(jnp.int32, (focus, wide), 1) // (wide // gangs)
    same = (head_row == head_col).astype(F32).astype(BF16)
    high = rated.astype(BF16)
    middle = (rated - high.astype(F32)).astype(BF16)
    low = (rated - high.astype(F32) - middle.astype(F32)).astype(BF16)
    rate = jnp.dot(high, same, preferred_element_type=F32)
    rate += jnp.dot(middle, same, preferred_element_type=F32)
    rate += jnp.dot(low, same, preferred_element_type=F32)
    rate_ref[...] = rate.astype(BF16)


def student_part(x, w, s, content, rating, wide, me, pieces, halves, order):
    requests, cand, feats = x.shape
    units = w.shape[1]
    rows = requests * cand
    return pl.pallas_call(
        functools.partial(student_kernel, requests, feats // pieces, order),
        out_shape=(jax.ShapeDtypeStruct((feats // halves, units), F32),) * halves
        + (
            jax.ShapeDtypeStruct((1, units), F32),
            jax.ShapeDtypeStruct((content.shape[0], wide), BF16),
        ),
        in_specs=[scalars()] + [full_vmem()] * 5,
        out_specs=(full_vmem(),) * (halves + 2),
        scratch_shapes=[VMEM((rows, units), BF16)] * 2,
        compiler_params=room(20),
        cost_estimate=pl.CostEstimate(
            flops=4 * requests * cand * feats * units, bytes_accessed=8 * 10**6, transcendentals=0
        ),
    )(me, x.reshape(rows, feats), w, s.reshape(1, units), content, rating.reshape(1, -1))


def block_scores(dims, me, payload, ask, look, rate):
    requests, hist_slots, kept, tops, gangs = dims
    focus = look.shape[0]
    span = look.shape[1] // gangs
    hist_rows, kept_rows, pieces, meta_at = rows_of(
        requests, hist_slots, kept, ask.shape[0], focus
    )
    hist = payload[:hist_rows, :]
    keys = jnp.dot(hist, look[...], preferred_element_type=F32).astype(BF16)
    values = jnp.dot(hist, rate[...], preferred_element_type=F32)
    queries = None
    for p in range(pieces):
        rows = payload[hist_rows + p * kept_rows : hist_rows + (p + 1) * kept_rows, :]
        part = jnp.dot(rows, ask[p * focus : (p + 1) * focus, :], preferred_element_type=F32)
        queries = part if queries is None else queries + part
    queries = (queries * span**-0.5).astype(BF16)
    wide = gangs * kept
    head_row = lax.broadcasted_iota(jnp.int32, (wide, look.shape[1]), 0) // kept
    head_col = lax.broadcasted_iota(jnp.int32, (wide, look.shape[1]), 1) // span
    same_head = head_row == head_col
    slot = lax.broadcasted_iota(jnp.int32, (hist_slots, wide), 0).astype(F32)
    meta = payload[meta_at : meta_at + META_ROWS, :].astype(F32)
    meta_lane = lax.broadcasted_iota(jnp.int32, meta.shape, 1)
    hit = jnp.where((meta_lane < tops) & (meta == me.astype(F32)), 1.0, 0.0)
    routed = jnp.max(hit, axis=-1, keepdims=True)
    lengths = jnp.sum(jnp.where(meta_lane == tops, meta, 0.0), axis=-1, keepdims=True)
    lane = lax.broadcasted_iota(jnp.int32, (1, kept_rows), 1) // kept
    scores = jnp.zeros((1, kept_rows), F32)
    for r in range(requests):
        q = queries[r * kept : (r + 1) * kept, :]
        q_wide = jnp.where(same_head, jnp.concatenate([q] * gangs, axis=0), jnp.zeros((), BF16))
        logits = lax.dot_general(
            keys[r * hist_slots : (r + 1) * hist_slots, :],
            q_wide,
            (((1,), (1,)), ((), ())),
            preferred_element_type=F32,
        )
        weights = jnp.where(slot < lengths[r : r + 1, :], jnp.exp(logits), 0.0)
        whole = jnp.sum(weights, axis=0, keepdims=True)
        level = jnp.where(whole > 1.0, 2.0**-64, 2.0**64)
        mixed = (weights * level) * values[r * hist_slots : (r + 1) * hist_slots, :]
        per_head = jnp.sum(mixed, axis=0, keepdims=True) / (whole * level)
        folded = per_head[:, :kept_rows]
        for b in range(1, wide // kept_rows):
            folded = folded + per_head[:, b * kept_rows : (b + 1) * kept_rows]
        shift = kept
        while shift < kept_rows:
            folded = folded + pltpu.roll(folded, shift, 1)
            shift *= 2
        scores = jnp.where((lane == r) & (routed[r : r + 1, :] > 0), folded, scores)
    return scores


def own_columns(me, rows_of_piece, sel_rows):
    focus = rows_of_piece[0].shape[1]
    own = None
    for p, rows in enumerate(rows_of_piece):
        feature = lax.broadcasted_iota(jnp.int32, (sel_rows, focus), 1) + p * focus
        wanted = lax.broadcasted_iota(jnp.int32, (sel_rows, focus), 0) + me * sel_rows
        pick = (feature == wanted).astype(F32).astype(BF16)
        got = lax.dot_general(pick, rows, (((1,), (1,)), ((), ())), preferred_element_type=F32)
        own = got if own is None else own + got
    return own.astype(BF16)


def rank_kernel(dims, sel_rows, layout, wants, first, info_ref, *refs):
    want_scores, want_hidden, parts = wants
    requests, hist_slots, kept, _, _ = dims
    n_in = sum(sum(pieces) for pieces in layout) if layout else 1
    arrays, refs = refs[:n_in], refs[n_in:]
    if want_scores:
        (a_ref, l_ref, r_ref), refs = refs[:3], refs[3:]
    if want_hidden:
        w_ref, refs = refs[0], refs[1:]
    if parts is not None:
        earlier, gs_ref, refs = refs[: len(parts)], refs[len(parts)], refs[len(parts) + 1 :]
    if want_scores:
        o_ref, refs = refs[0], refs[1:]
    if want_hidden:
        h_ref, s_ref, refs = refs[0], refs[1], refs[2:]
    buf, sems = refs
    blocks, _, focus = buf.shape
    feats = (a_ref if want_scores else w_ref).shape[0]
    hist_rows, kept_rows, pieces, _ = rows_of(requests, hist_slots, kept, feats, focus)
    low = 0 if want_scores else hist_rows
    high = low + buf.shape[1]

    def start_block(b):
        if not layout:
            fetch(arrays[0].at[b, pl.ds(low, high - low), :], buf.at[b], sems.at[b])
            return
        at, i = 0, sum(sum(pieces) for pieces in layout[:b])
        for choices in layout[b]:
            rows = arrays[i].shape[0]
            begin, end = max(at, low), min(at + rows, high)
            if begin < end:
                for choice in range(choices):

                    def start(array=arrays[i + choice], at=at, begin=begin, end=end):
                        fetch(
                            array.at[pl.ds(begin - at, end - begin), :],
                            buf.at[b, pl.ds(begin - low, end - begin), :],
                            sems.at[b],
                        )

                    if choices == 1:
                        start()
                    else:
                        pl.when(info_ref[3] == choice)(start)
            at += rows
            i += choices

    def wait_block(b):
        pltpu.make_async_copy(buf.at[b], buf.at[b], sems.at[b]).wait()

    for b in range(blocks):
        start_block(b)
    if parts is not None:
        slot = 0
        for ref, count in zip(earlier, parts):
            for b in range(count):
                o_ref[pl.ds(info_ref[1] ^ slot, 1), :] = ref[b]
                slot += 1
        scored, lanes = slot + blocks, o_ref.shape[1]
        for i in range(o_ref.shape[0] - scored):
            o_ref[scored + i : scored + i + 1, :] = gs_ref[:, i * lanes : (i + 1) * lanes]
    me = info_ref[0]
    if want_scores:

        def one(b, carry):
            wait_block(b)
            row = block_scores(dims, me, buf.at[b], a_ref, l_ref, r_ref)
            if parts is not None:
                o_ref[pl.ds(info_ref[1] ^ (first + b), 1), :] = row
            else:
                o_ref[b] = row
            return carry

        lax.fori_loop(0, blocks, one, 0)
    else:
        for b in range(blocks):
            wait_block(b)
    if want_hidden:
        rows_of_piece = []
        for p in range(pieces):
            at = hist_rows - low + p * kept_rows
            rows_of_piece.append(
                jnp.concatenate([buf[b, at : at + kept_rows, :] for b in range(blocks)], axis=0)
            )
        preact = None
        for p, rows in enumerate(rows_of_piece):
            part = jnp.dot(
                rows, w_ref[p * focus : (p + 1) * focus, :], preferred_element_type=F32
            )
            preact = part if preact is None else preact + part
        h_ref[...] = jnp.maximum(preact, 0.0).astype(BF16)
        s_ref[...] = own_columns(me, rows_of_piece, sel_rows)


def rank(dims, me, payloads, score_weights, hidden_weights, sel_rows, first=0, message=None):
    requests, _, kept, _, _ = dims
    kept_rows = requests * kept
    want_scores, want_hidden = score_weights is not None, hidden_weights is not None
    if isinstance(payloads, list):
        blocks = len(payloads)
        payloads = [[p if isinstance(p, tuple) else (p,) for p in block] for block in payloads]
        layout = [[len(p) for p in block] for block in payloads]
        arrays = [a for block in payloads for p in block for a in p]
        rows, focus = sum(p[0].shape[0] for p in payloads[0]), arrays[0].shape[1]
    else:
        blocks, rows, focus = payloads.shape
        layout, arrays = None, [payloads]
    if not want_scores:
        rows = kept_rows * (hidden_weights[0].shape[0] // focus)
    scratch = [VMEM((blocks, rows, focus), BF16), pltpu.SemaphoreType.DMA((blocks,))]
    weights = list(score_weights or ()) + list(hidden_weights or ())
    shapes, outs, small, parts = [], [], [], None
    if want_scores:
        if message is None:
            shapes.append(jax.ShapeDtypeStruct((blocks, 1, kept_rows), F32))
        else:
            earlier, gs = message
            parts = [e.shape[0] for e in earlier]
            small = list(earlier) + [gs]
            total = sum(parts) + blocks + gs.shape[1] // kept_rows
            shapes.append(jax.ShapeDtypeStruct((total, kept_rows), F32))
        outs.append(full_vmem())
    if want_hidden:
        units = hidden_weights[0].shape[1]
        shapes.append(jax.ShapeDtypeStruct((blocks * kept_rows, units), BF16))
        shapes.append(jax.ShapeDtypeStruct((sel_rows, blocks * kept_rows), BF16))
        outs += [full_vmem()] * 2
    flops = blocks * (7 * 10**8 * want_scores + 3 * 10**8 * want_hidden)
    return pl.pallas_call(
        functools.partial(
            rank_kernel, dims, sel_rows, layout, (want_scores, want_hidden, parts), first
        ),
        out_shape=tuple(shapes),
        in_specs=[scalars()]
        + [in_place()] * len(arrays)
        + [full_vmem()] * (len(weights) + len(small)),
        out_specs=tuple(outs),
        scratch_shapes=scratch,
        compiler_params=room(18),
        cost_estimate=pl.CostEstimate(
            flops=flops, bytes_accessed=blocks * 10**6, transcendentals=0
        ),
    )(me, *arrays, *weights, *small)


def target_kernel(kept, tops, n_parts, me_ref, got_ref, s_ref, base_ref, *refs):
    sel_refs, hid_refs = refs[:n_parts], refs[n_parts : 2 * n_parts]
    out_ref, short_ref, target_ref = refs[2 * n_parts :]
    kept_rows = got_ref.shape[1]
    units = s_ref.shape[1]
    blocks = got_ref.shape[0] - units // kept_rows
    sel_rows = sel_refs[0].shape[0]
    total = got_ref[...]
    exp_teacher = jnp.exp(total[:blocks, :] / tops)
    near = lax.broadcasted_iota(jnp.int32, (kept_rows, kept_rows), 0) // kept
    far = lax.broadcasted_iota(jnp.int32, (kept_rows, kept_rows), 1) // kept
    group = (near == far).astype(F32)
    sums = jnp.dot(
        exp_teacher, group, preferred_element_type=F32, precision=lax.Precision.HIGHEST
    )
    target_ref[...] = exp_teacher / sums
    grad = jnp.zeros((sel_rows, units), F32)
    lift = jnp.zeros((1, units), F32)
    slot = 0
    for sel_ref, hid_ref in zip(sel_refs, hid_refs):
        count = sel_ref.shape[1] // kept_rows
        target = jnp.concatenate(
            [target_ref[pl.ds(me_ref[1] ^ (slot + b), 1), :] for b in range(count)], axis=1
        )
        high = target.astype(BF16).astype(F32)
        hidden = hid_ref[...]
        slot += count
        live = jnp.where(hidden > 0, jnp.ones((), BF16), jnp.zeros((), BF16))
        scaled = sel_ref[...].astype(F32) * target
        upper = scaled.astype(BF16)
        lower = (scaled - upper.astype(F32)).astype(BF16)
        halves = jnp.dot(
            jnp.concatenate([upper, lower], axis=0), live, preferred_element_type=F32
        )
        grad += halves[:sel_rows, :] + halves[sel_rows:, :]
        both = jnp.concatenate([high, target - high], axis=0).astype(BF16)
        pair = jnp.dot(both, hidden, preferred_element_type=F32)
        lift += pair[0:1, :] + pair[1:2, :]
    out_ref[:sel_rows, :] = -grad * s_ref[...].astype(F32)
    held = base_ref.shape[0]
    at = pl.ds(pl.multiple_of(me_ref[2] * held, 8), held)
    out_ref[at, :] = out_ref[at, :] + base_ref[...]
    for i in range(units // kept_rows):
        at = slice(i * kept_rows, (i + 1) * kept_rows)
        out_ref[sel_rows : sel_rows + 1, at] = total[blocks + i : blocks + i + 1, :] - lift[:, at]
    out_ref[sel_rows + 1 :, :] = jnp.zeros((out_ref.shape[0] - sel_rows - 1, units), F32)
    row = out_ref[sel_rows : sel_rows + 1, :]
    short_ref[...] = out_ref[...].astype(BF16)
    short_ref[sel_rows + 1 : sel_rows + 2, :] = (row - row.astype(BF16).astype(F32)).astype(BF16)


def target_part(kept, tops, me, got, hiddens, owns, s, base):
    sel_rows = owns[0].shape[0]
    units = hiddens[0].shape[1]
    blocks = got.shape[0] - units // got.shape[1]
    parts = len(hiddens)
    return pl.pallas_call(
        functools.partial(target_kernel, kept, tops, parts),
        out_shape=tuple(jax.ShapeDtypeStruct((sel_rows + 8, units), t) for t in (F32, BF16)),
        in_specs=[scalars()] + [full_vmem()] * (3 + 2 * parts),
        out_specs=(full_vmem(),) * 2,
        scratch_shapes=[VMEM((blocks, got.shape[1]), F32)],
        compiler_params=room(18),
        cost_estimate=pl.CostEstimate(flops=10**9, bytes_accessed=6 * 10**6, transcendentals=0),
    )(me, got, s.reshape(1, units), base, *owns, *hiddens)


def along(pairs):
    table = []
    for z, z_to in pairs:
        for low in range(4):
            table.append((4 * z + low, 4 * z_to + low))
    return table


def flip(bits):
    return [(i, i ^ bits) for i in range(16)]


SIBLING, Y_OVER, Z_NEAR, Z_FAR = flip(1), flip(2), flip(4), flip(8)
Z_INNER = along([(1, 2), (2, 1)])
Z_OUT = along([(1, 0), (2, 3)])


def shift(x, table, axis="shard"):
    return lax.ppermute(x, axis, table)


def gather_stages(b, inner, cut):
    near = shift(b, Z_NEAR)
    over = shift(b, Y_OVER)
    mid = shift(b, Z_INNER)
    mid_far = shift(near, Z_INNER)
    out_far = shift(mid, Z_OUT)
    over_near = shift(near, Y_OVER)
    far = jnp.where(inner, mid_far, out_far)
    out_last = shift(mid_far, Z_OUT)
    over_far = shift(far, Y_OVER)
    last = [jnp.where(inner, mid[:cut], out_last[:cut]), jnp.where(inner, mid[cut:], out_last[cut:])]
    over_last = shift(last[0], Y_OVER)
    rest_out = shift(over_far[cut:], Z_OUT)
    rest_mid = shift(over[cut:], Z_INNER)

    def beside(p):
        if isinstance(p, tuple):
            return tuple(shift(a, SIBLING) for a in p)
        return shift(p, SIBLING)

    def both(*pieces):
        return [list(pieces), [beside(p) for p in pieces]]

    return [
        both(b) + both(over) + both(near),
        both(over_near) + both(far),
        both(over_far) + both(*last),
        both(over_last, (rest_out, rest_mid)),
    ]


def halving_order(block, me):
    away = block ^ me
    z1, z0, y, core, grp = [(away >> i) & 1 for i in (4, 3, 2, 1, 0)]
    return (core << 4) | (grp << 3) | (z0 << 2) | (y << 1) | z1


def halve(keep, sent):
    for table, axis in (
        (SIBLING, "shard"),
        ([(0, 1), (1, 0)], "group"),
        (Z_NEAR, "shard"),
        (Y_OVER, "shard"),
        (Z_FAR, "shard"),
    ):
        wide = axis == "group" or table is SIBLING
        got = shift(sent if wide else sent.astype(BF16), table, axis).astype(F32)
        half = keep.shape[0] // 2
        if table is Z_FAR:
            return keep + got
        keep, sent = keep[:half] + got[:half], keep[half:] + got[half:]


def sum_over_shard(x):
    for table in (SIBLING, Y_OVER):
        got = shift(x, table)
        x = x + got
    near, far, last = shift(x, Z_NEAR), shift(x, Z_FAR), shift(x, flip(12))
    return (x + near) + (far + last)


def sum_kernel(a_ref, b_ref, grad_ref, score_ref):
    rows = grad_ref.shape[0]
    grad_ref[...] = a_ref[:rows, :] + b_ref[:rows, :].astype(F32)
    pair = b_ref[rows : rows + 2, :].astype(F32)
    score_ref[...] = a_ref[rows : rows + 1, :] + (pair[0:1, :] + pair[1:2, :])


def sum_two(a, b, rows):
    return pl.pallas_call(
        sum_kernel,
        out_shape=(
            jax.ShapeDtypeStruct((rows, a.shape[1]), F32),
            jax.ShapeDtypeStruct((1, a.shape[1]), F32),
        ),
        in_specs=[full_vmem()] * 2,
        out_specs=(full_vmem(),) * 2,
        compiler_params=room(4),
    )(a, b)


def body(
    offer_attribute_matrix,
    kept_offers,
    expert_target,
    sequence_extent,
    behaviour_sequence,
    inner_projection_matrix,
    student_rating_vector,
    asking_matrix,
    lookup_matrix,
    content_matrix,
    expert_rating_vector,
):
    requests, _, feats = offer_attribute_matrix.shape
    kept = kept_offers.shape[1]
    hist_slots, _ = behaviour_sequence.shape[1:]
    tops = expert_target.shape[1]
    units = inner_projection_matrix.shape[1]
    n_shard = lax.axis_size("shard")
    sel_rows = feats // n_shard
    me = lax.axis_index("shard")
    n_group = lax.axis_size("group")
    grp = lax.axis_index("group")

    payload = pack(
        offer_attribute_matrix, kept_offers, behaviour_sequence, expert_target, sequence_extent
    )
    linked = n_shard == 16 and n_group == 2
    place = (me * n_group + grp if linked else me).astype(jnp.int32).reshape(1)
    stack = (
        offer_attribute_matrix,
        inner_projection_matrix,
        student_rating_vector,
        content_matrix[0],
        expert_rating_vector[0],
        ATTENDER_GANGS * kept,
        place,
    )
    if linked:
        inner = ((me >> 2) ^ (me >> 3)) & 1
        stages = gather_stages(payload, inner == 1, requests * hist_slots + META_ROWS)
        keep, sent, gs_student, rate = student_part(
            *stack, n_shard * n_group, 2, halving_order
        )
        base = halve(keep, sent)
        info = jnp.stack([me, me, grp, inner]).astype(jnp.int32)
    else:
        payloads = lax.all_gather(payload, "shard", axis=0, tiled=False)
        stages = [payloads[b : b + 4] for b in range(0, n_shard, 4)]
        grad_student, gs_student, rate = student_part(
            *stack, n_shard, 1, lambda block, at: block
        )
        base = lax.psum_scatter(grad_student, "shard", scatter_dimension=0, tiled=True)
        info = jnp.stack([me, 0 * me, 0 * me, 0 * me]).astype(jnp.int32)

    dims = (requests, hist_slots, kept, tops, ATTENDER_GANGS)
    score_weights = (asking_matrix[0], lookup_matrix[0], rate)
    hidden_weights = (inner_projection_matrix,)
    scores, hiddens, owns = [], [], []
    for stage in stages[:-1]:
        score, hidden, own = rank(dims, info, stage, score_weights, hidden_weights, sel_rows)
        hiddens.append(hidden)
        owns.append(own)
        scores.append(score)
    known = sum(s.shape[0] for s in scores)
    (send,) = rank(
        dims, info, stages[-1], score_weights, None, sel_rows, known, (scores, gs_student)
    )
    hidden, own = rank(dims, info, stages[-1], None, hidden_weights, sel_rows)
    hiddens.append(hidden)
    owns.append(own)
    got = sum_over_shard(send) if linked else lax.psum(send, "shard")
    mine, short = target_part(kept, tops, info, got, hiddens, owns, student_rating_vector, base)
    if linked:
        grad, lift = sum_two(mine, shift(short, [(0, 1), (1, 0)], "group"), sel_rows)
        return grad, lift.reshape(units)
    whole = lax.psum(mine, "group")
    return whole[:sel_rows], whole[sel_rows]


def solution(mesh):
    placed = (
        P(("group", "shard"), None, None),
        P(("group", "shard"), None),
        P(("group", "shard"), None),
        P(("group", "shard")),
        P(("group", "shard"), None, None),
        P(),
        P(),
        P("shard", None, None),
        P("shard", None, None),
        P("shard", None, None),
        P("shard", None),
    )
    return jax.shard_map(
        body, mesh=mesh, in_specs=placed, out_specs=(P("shard", None), P()), check_vma=False
    )
```
